32 devices in a mesh: dp: 4 (over y, x), token: 8 (over z, core).
Axes of the slice: x: 2, y: 2, z: 4, core: 2. Of those that a mesh axis runs over, the one named last changes fastest.
Arguments:
- mix_input: bfloat16 [1536, 8, 768], P('dp', 'token'), may hold values from -6 to 6
- out_grad: bfloat16 [1536, 8, 768], P('dp', 'token'), may hold values from -1.5 to 1.5
- w_up: bfloat16 [8, 768, 3072], P('token'), may hold values from -0.21875 to 0.21875
- w_down: bfloat16 [8, 3072, 768], P('token'), may hold values from -0.109375 to 0.109375
- gain_first: float32 [8, 768], P('token'), may hold values from 0.25 to 1.75
- gain_second: float32 [8, 768], P('token'), may hold values from 0.25 to 1.75
- owner_dev: int32 [8, 1536, 1], P('token', 'dp'), may hold values from 0 to 3; in each aligned block of 384 rows (0 to 383, 384 to 767, ..., all dimensions but the last counted through in order) at most 240 rows name the same one
- slot_row: int32 [8, 1536], P('token', 'dp'), may hold values from 0 to 255
Outputs:
- grad_up: float32 [8, 768, 3072], P('token', 'dp')
- grad_down: float32 [8, 3072, 768], P('token', 'dp')
- row_grad: float32 [8, 1024, 768], P('token', 'dp')
The draws below stay inside these ranges and needn't reach their ends.
Inputs may be any that keep to these rules, and one draw needn't show every extreme that they name: `owner_dev`: in the rows of one device (aligned blocks of 384 samples of one token) no owner is named by more than 240 rows, a bound that some block reaches.
All inputs are finite; a program needn't handle non-finite values.
Results may differ from the reference program's by a relative error of at most 0.015.
Values may be sent and summed in bfloat16 or wider, within the bound.
A program may use at most 128 MiB of HBM per device.

```python
import math
import jax
import jax.numpy as jnp
import numpy as np
from jax import lax

D = 768
F = 3072
B_DEV = 384
HOT = 256
NTOK = 8
HS = 96
BATCH = 1536
CAP = 240
N_DP = 4


def touch_ends(result, own_key, smallest, top_value):
    longest = result.shape.index(max(result.shape))
    spots = []
    for shift in (0, 1):
        where = [jax.random.randint(jax.random.fold_in(own_key, axis), (), 0, length) for axis, length in enumerate(result.shape)]
        where[longest] = (where[longest] + shift) % result.shape[longest]
        spots.append(tuple(where))
    return result.at[spots[0]].set(smallest).at[spots[1]].set(top_value)


def shard_levels(own_key, dims, shards, low, largest):
    factor_of, own = 1.0, jax.random.fold_in(own_key, 6)
    for dim, blocks in shards:
        steps = jnp.exp(jax.random.uniform(jax.random.fold_in(own, dim), (blocks,), jnp.float32, low / len(shards), largest / len(shards)))
        factor_of = factor_of * jnp.repeat(steps, dims[dim] // blocks).reshape([-1 if axis == dim else 1 for axis in range(len(dims))])
    return factor_of


def rank_table(amount, slope):
    weights = [(1 << 20) // math.isqrt(rank ** slope) + 1 for rank in range(1, amount + 1)]
    spread = 1 + sum(weights) // (1 << 30)
    return np.cumsum(np.array([max(1, weight // spread) for weight in weights]))


def ranked_ids(own_key, dims, number_of, slope):
    grid = rank_table(number_of, slope)
    ticket = jax.random.randint(jax.random.fold_in(own_key, 1), dims, 0, int(grid[number_of - 1]))
    grade = jnp.searchsorted(jnp.asarray(grid, jnp.int32), ticket, side="right")
    return jax.random.permutation(jax.random.fold_in(own_key, 2), number_of)[grade].astype(jnp.int32)


def shared_out(stream_key, own, number, rows, number_of, top, limit, lean):
    sequence = jax.random.permutation(stream_key, number_of)
    crowded, ordinary = portions_of(number_of, rows * top, limit, lean, True), portions_of(number_of, rows * top, limit, lean, False)
    places = jnp.arange(number_of)

    def named(tallies, turn):
        used = int((tallies > 0).sum())
        fixed = max(1, used // 4)
        shifted = fixed + (places - fixed + turn * (used - fixed)) % max(1, number_of - fixed)
        return jnp.zeros((number_of,), jnp.int32).at[sequence[jnp.where(places < fixed, places, shifted)]].set(jnp.asarray(tallies, jnp.int32))

    tallies = jnp.where(number % 4 == 0, named(crowded, number // 4), named(ordinary, number - number // 4 - 1))
    mixed = jax.random.permutation(jax.random.fold_in(own, 3), number_of)
    donor, sink = mixed[0:number_of // 2 * 2:2], mixed[1:number_of // 2 * 2:2]
    margin = jnp.minimum(tallies[donor] - 1, limit - tallies[sink]) // 2
    margin = jnp.where((donor == sequence[0]) | (sink == sequence[0]) | (tallies[sink] == 0), 0, jnp.maximum(margin, 0))
    shifted = jax.random.randint(jax.random.fold_in(own, 4), (number_of // 2,), 0, 1 << 20) % (margin + 1)
    tallies = tallies.at[donor].add(-shifted).at[sink].add(shifted)
    labels = jnp.searchsorted(jnp.cumsum(tallies), jnp.arange(rows * top), side="right").astype(jnp.int32)
    grid = labels.reshape(top, rows).T
    grid = grid[jax.random.permutation(jax.random.fold_in(own, 1), rows)]
    turn = jax.random.randint(jax.random.fold_in(own, 2), (rows, 1), 0, top)
    return jnp.take_along_axis(grid, (jnp.arange(top)[None, :] + turn) % top, axis=1)


def portions_of(count, total, limit, slope, full):
    portions = [(1 << 20) // math.isqrt(standing ** slope) + 1 for standing in range(1, count + 1)]
    largest = limit if full else min(limit, max(-(-total // count), total * portions[0] // sum(portions)))
    least = 1 if total - largest >= count - 1 else 0
    counts, rest = [largest] + [least] * (count - 1), total - largest - least * (count - 1)
    while rest > 0:
        candidates = [i for i in range(1, count) if counts[i] < largest] or [i for i in range(1, count) if counts[i] < limit]
        pool, remaining = sum([portions[i] for i in candidates]), rest
        for i in candidates:
            addition = min(limit - counts[i], max(1, remaining * portions[i] // pool), rest)
            counts[i] = counts[i] + addition
            rest = rest - addition
    return np.array(counts)


def centred(key, extent, deviation, limit, split=(), dtype=jnp.bfloat16):
    entries = jax.random.normal(key, extent, jnp.float32) * deviation
    if len(split) > 0:
        entries = shard_levels(key, extent, split, -0.22, 0.18) * entries
    return jnp.clip(entries, min=-limit, max=limit).astype(dtype)


def setup_inputs(seed: int = 0) -> dict:
    streams_of = jax.random.split(jax.random.key(seed), 9)
    mix_input = centred(streams_of[0], (BATCH, NTOK, D), 1.0, 6.0, ((0, 4), (1, 8)))
    out_grad = centred(streams_of[1], (BATCH, NTOK, D), 0.25, 1.5, ((0, 4), (1, 8)))
    w_up = centred(streams_of[2], (NTOK, D, F), D ** -0.5, 0.21875, ((0, 8),))
    w_down = centred(streams_of[3], (NTOK, F, D), F ** -0.5, 0.109375, ((0, 8),))
    gain_first = jnp.clip(1.0 + 0.15 * jax.random.normal(streams_of[4], (NTOK, D), jnp.float32), 0.25, 1.75)
    gain_second = jnp.clip(1.0 + 0.15 * jax.random.normal(streams_of[5], (NTOK, D), jnp.float32), 0.25, 1.75)
    owner_dev_keys = jax.random.split(jax.random.fold_in(streams_of[6], 1), NTOK * BATCH // B_DEV)
    owner_dev_turns = jax.random.permutation(jax.random.fold_in(streams_of[6], 3), NTOK * BATCH // B_DEV)
    owner_dev = jax.vmap(lambda own, number: shared_out(jax.random.fold_in(streams_of[6], 2), own, number, B_DEV, N_DP, 1, CAP, 2))(owner_dev_keys, owner_dev_turns).reshape((NTOK, BATCH, 1))
    slot_row = touch_ends(ranked_ids(streams_of[7], (NTOK, BATCH), HOT, 2), jax.random.fold_in(streams_of[7], 3), 0, HOT - 1).astype(jnp.int32)
    return dict(mix_input=mix_input, out_grad=out_grad, w_up=w_up, w_down=w_down, gain_first=gain_first, gain_second=gain_second, owner_dev=owner_dev, slot_row=slot_row)


EPS = 1e-05
HALF_ROOT = 0.7071067811865476
INV_ROOT_TAU = 0.3989422804014327

def normalize(values):
    center = values - lax.optimization_barrier(jnp.mean(values, axis=-1, keepdims=True))
    inv_scale = lax.rsqrt(lax.optimization_barrier(jnp.mean(center * center, axis=-1, keepdims=True)) + EPS)
    return (center * inv_scale, inv_scale)

def norm_back(grad_norm, normed, inv_scale):
    mean_grad = lax.optimization_barrier(jnp.mean(grad_norm, axis=-1, keepdims=True))
    mean_proj = lax.optimization_barrier(jnp.mean(grad_norm * normed, axis=-1, keepdims=True))
    return inv_scale * (grad_norm - mean_grad - normed * mean_proj)

def gelu_parts(pre_act):
    cumul = 0.5 * (1.0 + jax.scipy.special.erf(pre_act * HALF_ROOT))
    density = jnp.exp(-0.5 * pre_act * pre_act) * INV_ROOT_TAU
    return (pre_act * cumul, cumul + pre_act * density)

def group_partial(left, right):
    left_parts = left.reshape(N_DP, B_DEV, left.shape[1]).astype(jnp.float32)
    right_parts = right.reshape(N_DP, B_DEV, right.shape[1]).astype(jnp.float32)
    partial_sums = jnp.einsum('nba,nbc->nac', left_parts, right_parts).astype(jnp.bfloat16)
    partial_sums = lax.optimization_barrier(partial_sums)
    return lax.optimization_barrier(jnp.sum(partial_sums.astype(jnp.float32), axis=0))

def per_token(inputs):
    mix_slab, grad_slab, up_mat, down_mat, gain_one, gain_two = inputs
    normed, inv_scale = normalize(mix_slab.astype(jnp.float32))
    hidden_in = (normed * gain_one).astype(jnp.bfloat16)
    pre_act = jnp.dot(hidden_in, up_mat, preferred_element_type=jnp.float32)
    act_value, act_slope = gelu_parts(pre_act)
    active = act_value.astype(jnp.bfloat16)
    outer_sum = jnp.dot(active, down_mat, preferred_element_type=jnp.float32) + hidden_in.astype(jnp.float32)
    normed_out, inv_out = normalize(outer_sum)
    grad_wide = norm_back(grad_slab.astype(jnp.float32) * gain_two, normed_out, inv_out)
    grad_mid = grad_wide.astype(jnp.bfloat16)
    grad_act = jnp.dot(grad_mid, down_mat.T, preferred_element_type=jnp.float32)
    grad_pre = (grad_act * act_slope).astype(jnp.bfloat16)
    grad_up = group_partial(hidden_in, grad_pre)
    grad_down = group_partial(active, grad_mid)
    grad_hidden = jnp.dot(grad_pre, up_mat.T, preferred_element_type=jnp.float32) + grad_wide
    grad_sum = norm_back(grad_hidden * gain_one, normed, inv_scale).astype(jnp.bfloat16)
    return (grad_up, grad_down, grad_sum)

def reference(mix_input, out_grad, w_up, w_down, gain_first, gain_second, owner_dev, slot_row):
    mix_tok = jnp.swapaxes(mix_input, 0, 1)
    grad_tok = jnp.swapaxes(out_grad, 0, 1)
    grad_up, grad_down, grad_sum = lax.map(per_token, (mix_tok, grad_tok, w_up, w_down, gain_first, gain_second))
    pieces = grad_sum.reshape(NTOK, BATCH, NTOK, HS)
    swapped = jnp.transpose(pieces, (2, 1, 0, 3)).reshape(NTOK, BATCH, D)
    embed_grad = (grad_sum.astype(jnp.float32) + swapped.astype(jnp.float32)).astype(jnp.bfloat16)
    target = owner_dev[:, :, 0] * HOT + slot_row

    def table_sum(grad_rows, target_rows):
        return jax.ops.segment_sum(grad_rows.astype(jnp.float32), target_rows, num_segments=N_DP * HOT)
    row_grad = jax.vmap(table_sum)(embed_grad, target)
    return (grad_up, grad_down, row_grad)
```

```python
import functools

import jax
import jax.numpy as jnp
from jax import lax
from jax.experimental import pallas as pl
from jax.experimental.pallas import tpu as pltpu

from jax.sharding import PartitionSpec as P

HOT = 256


EPS = 1e-05
HALF_ROOT = 0.7071067811865476
INV_ROOT_TAU = 0.3989422804014327


def normalize(values):
    center = values - jnp.mean(values, axis=-1, keepdims=True)
    inv_scale = lax.rsqrt(jnp.mean(center * center, axis=-1, keepdims=True) + EPS)
    return (center * inv_scale, inv_scale)


def norm_back(grad_norm, normed, inv_scale):
    mean_grad = jnp.mean(grad_norm, axis=-1, keepdims=True)
    mean_proj = jnp.mean(grad_norm * normed, axis=-1, keepdims=True)
    return inv_scale * (grad_norm - mean_grad - normed * mean_proj)


def gelu_parts(pre_act):
    cumul = 0.5 * (1.0 + jax.scipy.special.erf(pre_act * HALF_ROOT))
    density = jnp.exp(-0.5 * pre_act * pre_act) * INV_ROOT_TAU
    return (pre_act * cumul, cumul + pre_act * density)


def contract_rows(left, right):
    return lax.dot_general(
        left, right, (((0,), (0,)), ((), ())), preferred_element_type=jnp.float32
    )


def contract_cols(left, right):
    return lax.dot_general(
        left, right, (((1,), (1,)), ((), ())), preferred_element_type=jnp.float32
    )


def per_device(mix_input, out_grad, w_up, w_down, gain_first, gain_second, owner_dev, slot_row):
    batch_rows = mix_input.shape[0]
    width = mix_input.shape[2]
    owners = lax.axis_size("dp")
    normed, inv_scale = normalize(mix_input[:, 0, :].astype(jnp.float32))
    hidden_in = (normed * gain_first[0]).astype(jnp.bfloat16)
    pre_act = jnp.dot(hidden_in, w_up[0], preferred_element_type=jnp.float32)
    act_value, act_slope = gelu_parts(pre_act)
    active = act_value.astype(jnp.bfloat16)
    outer_sum = jnp.dot(active, w_down[0], preferred_element_type=jnp.float32) + hidden_in.astype(
        jnp.float32
    )
    normed_out, inv_out = normalize(outer_sum)
    grad_wide = norm_back(
        out_grad[:, 0, :].astype(jnp.float32) * gain_second[0], normed_out, inv_out
    )
    grad_mid = grad_wide.astype(jnp.bfloat16)
    grad_act = contract_cols(grad_mid, w_down[0])
    grad_pre = (grad_act * act_slope).astype(jnp.bfloat16)
    up_whole = contract_rows(hidden_in, grad_pre)
    down_whole = contract_rows(active, grad_mid)
    grad_up, grad_down = (
        lax.psum_scatter(
            up_whole.astype(jnp.bfloat16), "dp", scatter_dimension=0, tiled=True
        ).astype(jnp.float32),
        lax.psum_scatter(
            down_whole.astype(jnp.bfloat16), "dp", scatter_dimension=0, tiled=True
        ).astype(jnp.float32),
    )
    grad_hidden = contract_cols(grad_pre, w_up[0]) + grad_wide
    grad_sum = norm_back(grad_hidden * gain_first[0], normed, inv_scale).astype(jnp.bfloat16)
    pieces = lax.axis_size("token")
    swapped = lax.all_to_all(
        grad_sum.reshape(batch_rows, pieces, width // pieces),
        "token",
        split_axis=1,
        concat_axis=1,
        tiled=True,
    )
    embed_grad = (
        grad_sum.astype(jnp.float32) + swapped.reshape(batch_rows, width).astype(jnp.float32)
    ).astype(jnp.bfloat16)
    owner_ids = owner_dev[0, :, 0]
    slot_ids = slot_row[0]
    capacity = max(2, 8 * (5 * batch_rows // (16 * owners)))
    owner_hot = (
        owner_ids[:, None] == lax.broadcasted_iota(jnp.int32, (batch_rows, owners), 1)
    ).astype(jnp.int32)
    rank_within = jnp.sum((jnp.cumsum(owner_hot, axis=0) - 1) * owner_hot, axis=1)
    place = owner_ids * capacity + rank_within
    dispatch_mask = (
        lax.broadcasted_iota(jnp.int32, (owners * capacity, batch_rows), 0) == place[None, :]
    )
    send_grad = jnp.dot(
        dispatch_mask.astype(jnp.bfloat16), embed_grad, preferred_element_type=jnp.float32
    )
    send_grad = send_grad.astype(jnp.bfloat16).reshape(owners, capacity, width)
    send_slot = jnp.sum(dispatch_mask.astype(jnp.int32) * (slot_ids + 1)[None, :], axis=1) - 1
    send_slot = send_slot.astype(jnp.float32).astype(jnp.bfloat16).reshape(owners, capacity)
    recv_grad, recv_slot = (
        lax.all_to_all(send_grad, "dp", split_axis=0, concat_axis=0, tiled=True),
        lax.all_to_all(send_slot, "dp", split_axis=0, concat_axis=0, tiled=True),
    )
    slot_values = recv_slot.reshape(1, owners * capacity).astype(jnp.float32)
    gather_hot = (
        lax.broadcasted_iota(jnp.int32, (HOT, owners * capacity), 0).astype(jnp.float32)
        == slot_values
    ).astype(jnp.bfloat16)
    row_grad = jnp.dot(
        gather_hot, recv_grad.reshape(owners * capacity, width), preferred_element_type=jnp.float32
    )
    return (grad_up[None], grad_down[None], row_grad[None])


SUB = 256
VMEM_BYTES = 67043328
MESH = pl.DeviceIdType.MESH


def contract_flat(left, right):
    return jnp.dot(left, right, preferred_element_type=jnp.float32)


def fused_kernel(
    n_tok,
    mix_in, grad_in, up_in, down_in, gain1_in, gain2_in, owner_in, slot_in,
    gup_out, gdown_out, rows_out,
    mix_v, mid_v, h_v, up_v, down_v, slope_v, act_v, hsel_v, gup_v, gdown_v, wide_v, acc_v, grad_v,
    sum_v, swap_v, embed_v, far_v, part_v, back_v, mine_v, gain1_v, gain2_v, owner_v, slot_v,
    up_sem, down_sem, load_sem, out_sem, send_sem, recv_sem, swap_send, swap_recv,
):
    rows, width = grad_v.shape
    chunks, _, part = up_v.shape
    piece = width // n_tok
    half_w = width // 2
    half_r = rows // 2
    hot_rows = rows_out.shape[0]
    bf, f32 = jnp.bfloat16, jnp.float32
    me = lax.axis_index("dp")
    tok = lax.axis_index("token")
    col = lax.rem(me, 2)
    over_x = {"dp": me + 1 - 2 * col}
    over_y = {"dp": lax.rem(me + 2, 4)}

    def group(g):
        return pl.ds(g * rows, rows)

    def chunk_at(j):
        return lax.rem(j + me + 1, chunks)

    def remote(i, src, dst, device):
        return pltpu.make_async_remote_copy(
            src_ref=src, dst_ref=dst, send_sem=send_sem.at[i], recv_sem=recv_sem.at[i],
            device_id=device, device_id_type=MESH,
        )

    def load_up(j):
        c = chunk_at(j)
        cols = pl.ds(pl.multiple_of(c * part, part), part)
        return pltpu.make_async_copy(up_in.at[:, cols], up_v.at[c], up_sem.at[j])

    def load_down(j):
        c = chunk_at(j)
        lines = pl.ds(pl.multiple_of(c * part, part), part)
        return pltpu.make_async_copy(down_in.at[lines, :], down_v.at[c], down_sem.at[j])

    small = [
        (mix_in, mix_v.at[group(0)]),
        (gain1_in, gain1_v),
        (gain2_in, gain2_v),
        (grad_in, grad_v),
        (owner_in, owner_v.at[0]),
        (slot_in, slot_v.at[0]),
    ]
    loads = [pltpu.make_async_copy(s, d, load_sem.at[i]) for i, (s, d) in enumerate(small)]
    loads[0].start()
    loads[1].start()
    for j in range(chunks):
        load_up(j).start()
        load_down(j).start()
    for load in loads[2:]:
        load.start()

    barrier = pltpu.get_barrier_semaphore()
    for device in (over_x, over_y):
        pl.semaphore_signal(barrier, inc=1, device_id=device, device_id_type=MESH)
    for k in range(1, n_tok):
        peer = {"token": lax.rem(tok + k, n_tok)}
        pl.semaphore_signal(barrier, inc=1, device_id=peer, device_id_type=MESH)
    pl.semaphore_wait(barrier, n_tok + 1)

    mix_x = remote(0, mix_in, mix_v.at[group(1)], over_x)
    mix_y = remote(1, mix_in, mix_v.at[group(2)], over_y)
    ids = [
        remote(2, owner_in, owner_v.at[1], over_x),
        remote(3, slot_in, slot_v.at[1], over_x),
        remote(4, owner_in, owner_v.at[2], over_y),
        remote(5, slot_in, slot_v.at[2], over_y),
    ]
    for copy in [mix_x, mix_y] + ids:
        copy.start()

    def norm_group(g):
        normed, _ = normalize(mix_v[group(g), :].astype(f32))
        h_v[group(g), :] = (normed * gain1_v[...]).astype(bf)

    def pick_group(g):
        shape = (hsel_v.shape[0], width)
        row = lax.broadcasted_iota(jnp.int32, shape, 0) + me * shape[0]
        pick = (row == lax.broadcasted_iota(jnp.int32, shape, 1)).astype(bf)
        hsel_v[:, group(g)] = contract_cols(pick, h_v[group(g), :]).astype(bf)

    def activate(g, c):
        pres = [
            contract_flat(h_v[group(g), :], up_v[c, :, s : s + SUB]) for s in range(0, part, SUB)
        ]
        total = None
        for i, pre in enumerate(pres):
            cols = slice(i * SUB, (i + 1) * SUB)
            value, slope = gelu_parts(pre)
            act = value.astype(bf)
            act_v[group(g), cols] = act
            slope_v[c, group(g), cols] = slope.astype(bf)
            if g == 0:
                more = contract_flat(act, down_v[c, cols, :])
                total = more if total is None else total + more
        return total

    loads[0].wait()
    loads[1].wait()
    norm_group(0)
    acc_v[...] = h_v[group(0), :].astype(f32)

    @pl.loop(0, chunks)
    def _(j):
        load_up(j).wait()
        load_down(j).wait()
        acc_v[...] += activate(0, chunk_at(j))

    for load in loads[2:]:
        load.wait()
    normed, inv = normalize(acc_v[...])
    wide = norm_back(grad_v[...].astype(f32) * gain2_v[...], normed, inv)
    wide_v[...] = wide
    mid_v[group(0), :] = wide.astype(bf)
    mid_x = remote(6, mid_v.at[group(0)], mid_v.at[group(1)], over_x)
    mid_y = remote(7, mid_v.at[group(0)], mid_v.at[group(2)], over_y)
    mid_x.start()
    mid_y.start()

    def slope_group(g, c):
        grad_act = contract_cols(mid_v[group(g), :], down_v[c])
        grad_pre = (grad_act * slope_v[c, group(g), :].astype(f32)).astype(bf)
        slope_v[c, group(g), :] = grad_pre
        return grad_pre

    acc_v[...] = wide_v[...]

    @pl.loop(0, chunks)
    def _(c):
        acc_v[...] += contract_cols(slope_group(0, c), up_v[c])

    normed, inv = normalize(mix_v[group(0), :].astype(f32))
    grad_sum = norm_back(acc_v[...] * gain1_v[...], normed, inv)
    sum_v[...] = grad_sum.T.astype(bf)

    own_piece = pl.ds(pl.multiple_of(tok * piece, piece), piece)
    swaps = []
    for k in range(1, n_tok):
        peer = lax.rem(tok + k, n_tok)
        there = pl.ds(pl.multiple_of(peer * piece, piece), piece)
        swaps.append(
            pltpu.make_async_remote_copy(
                src_ref=sum_v.at[there], dst_ref=swap_v.at[own_piece],
                send_sem=swap_send.at[k - 1], recv_sem=swap_recv.at[k - 1],
                device_id={"token": peer}, device_id_type=MESH,
            )
        )
        swaps[-1].start()
    swap_v[own_piece, :] = sum_v[own_piece, :]

    first, second = pl.ds(0, half_r), pl.ds(half_r, half_r)

    def block(ref, g, part_of):
        return ref.at[pl.ds(g * rows + part_of * half_r, half_r)]

    mix_x.wait_recv()
    mix_dx = remote(8, block(mix_v, 1, 0), block(mix_v, 3, 0), over_y)
    mix_dx.start()
    mix_y.wait_recv()
    mix_dy = remote(9, block(mix_v, 2, 1), block(mix_v, 3, 1), over_x)
    mix_dy.start()

    def others(g):
        norm_group(g)
        pick_group(g)

        @pl.loop(0, chunks)
        def _(j):
            activate(g, chunk_at(j))

    pick_group(0)
    others(1)
    others(2)

    for copy in swaps:
        copy.wait_recv()
    embed_v[...] = (sum_v[...].astype(f32) + swap_v[...].astype(f32)).astype(bf)
    low, high = pl.ds(0, half_w), pl.ds(half_w, half_w)
    far_x = remote(10, embed_v.at[low], far_v.at[0], over_x)
    far_y = remote(11, embed_v.at[high], far_v.at[1], over_y)
    far_x.start()
    far_y.start()

    mid_x.wait_recv()
    mid_dx = remote(12, block(mid_v, 1, 0), block(mid_v, 3, 0), over_y)
    mid_dx.start()
    mid_y.wait_recv()
    mid_dy = remote(13, block(mid_v, 2, 1), block(mid_v, 3, 1), over_x)
    mid_dy.start()

    pair = pl.ds(0, 2 * rows)

    @pl.loop(0, chunks)
    def _(c):
        slope_group(1, c)
        gup_v[c] = contract_flat(hsel_v[:, pair], slope_v[c, pair, :])

    gdown_v[...] = contract_rows(act_v[pair, :], mid_v[pair, :])

    @pl.loop(0, chunks)
    def _(c):
        grad_pre = slope_group(2, c)
        gup_v[c] += contract_flat(hsel_v[:, group(2)], grad_pre)

    gdown_v[...] += contract_rows(act_v[group(2), :], mid_v[group(2), :])

    mix_dx.wait_recv()
    mix_dy.wait_recv()
    others(3)

    for copy in ids:
        copy.wait_recv()
    far_x.wait_recv()
    far_y.wait_recv()

    def hot(k, owner):
        target = owner_v[k] * hot_rows + slot_v[k]
        row = lax.broadcasted_iota(jnp.int32, (hot_rows, rows), 0) + owner * hot_rows
        return (row == target).astype(bf)

    def merge(owner, k, cols):
        kept = contract_cols(hot(0, owner), embed_v[cols, :])
        return kept + contract_cols(hot(k, owner), far_v[k - 1])

    part_v[0] = merge(over_y["dp"], 1, low).astype(bf)
    part_v[1] = merge(over_x["dp"], 2, high).astype(bf)
    back_y = remote(14, part_v.at[0], back_v.at[0], over_y)
    back_x = remote(15, part_v.at[1], back_v.at[1], over_x)
    back_y.start()
    back_x.start()
    mine_v[:, :half_w] = merge(me, 1, low)
    mine_v[:, half_w:] = merge(me, 2, high)

    mid_dx.wait_recv()
    mid_dy.wait_recv()

    def store_up(c):
        cols = pl.ds(pl.multiple_of(c * part, part), part)
        return pltpu.make_async_copy(gup_v.at[c], gup_out.at[:, cols], up_sem.at[c])

    @pl.loop(0, chunks)
    def _(c):
        grad_pre = slope_group(3, c)
        gup_v[c] += contract_flat(hsel_v[:, group(3)], grad_pre)
        store_up(c).start()

    gdown_v[...] += contract_rows(act_v[group(3), :], mid_v[group(3), :])
    store_down = pltpu.make_async_copy(gdown_v, gdown_out, out_sem.at[0])
    store_down.start()

    back_y.wait_recv()
    back_x.wait_recv()
    mine_v[:, :half_w] += back_v[0].astype(f32)
    mine_v[:, half_w:] += back_v[1].astype(f32)
    store_rows = pltpu.make_async_copy(mine_v, rows_out, out_sem.at[1])
    store_rows.start()

    for copy in [mix_x, mix_y] + ids + [mid_x, mid_y, mix_dx, mix_dy] + swaps:
        copy.wait_send()
    for copy in [far_x, far_y, mid_dx, mid_dy, back_x, back_y]:
        copy.wait_send()
    for c in range(chunks):
        store_up(c).wait()
    store_down.wait()
    store_rows.wait()


def small_group(mix_input, out_grad, w_up, w_down, gain_first, gain_second, owner_dev, slot_row):
    rows = mix_input.shape[0]
    width = mix_input.shape[2]
    hidden = w_up.shape[2]
    groups = lax.axis_size("dp")
    n_tok = lax.axis_size("token")
    part = hidden // groups
    own = width // groups
    half = width // 2
    bf, f32, i32 = jnp.bfloat16, jnp.float32, jnp.int32
    vm, dma = pltpu.VMEM, pltpu.SemaphoreType.DMA
    anywhere = pl.BlockSpec(memory_space=pl.ANY)
    unit = 2 * rows * width * hidden
    grad_up, grad_down, row_grad = pl.pallas_call(
        functools.partial(fused_kernel, n_tok),
        in_specs=[anywhere] * 8,
        out_specs=[anywhere] * 3,
        out_shape=[
            jax.ShapeDtypeStruct((own, hidden), f32),
            jax.ShapeDtypeStruct((part, width), f32),
            jax.ShapeDtypeStruct((HOT, width), f32),
        ],
        scratch_shapes=[
            vm((groups * rows, width), bf),
            vm((groups * rows, width), bf),
            vm((groups * rows, width), bf),
            vm((groups, width, part), bf),
            vm((groups, part, width), bf),
            vm((groups, groups * rows, part), bf),
            vm((groups * rows, part), bf),
            vm((own, groups * rows), bf),
            vm((groups, own, part), f32),
            vm((part, width), f32),
            vm((rows, width), f32),
            vm((rows, width), f32),
            vm((rows, width), bf),
            vm((width, rows), bf),
            vm((width, rows), bf),
            vm((width, rows), bf),
            vm((2, half, rows), bf),
            vm((2, HOT, half), bf),
            vm((2, HOT, half), bf),
            vm((HOT, width), f32),
            vm((1, width), f32),
            vm((1, width), f32),
            vm((3, 1, rows), i32),
            vm((3, 1, rows), i32),
            dma((groups,)),
            dma((groups,)),
            dma((6,)),
            dma((2,)),
            dma((16,)),
            dma((16,)),
            dma((n_tok - 1,)),
            dma((n_tok - 1,)),
        ],
        compiler_params=pltpu.CompilerParams(
            vmem_limit_bytes=VMEM_BYTES, collective_id=0, has_side_effects=True
        ),
        cost_estimate=pl.CostEstimate(
            flops=12 * unit, bytes_accessed=8 * width * hidden, transcendentals=0
        ),
        name="fused",
    )(
        mix_input[:, 0, :], out_grad[:, 0, :], w_up[0], w_down[0], gain_first, gain_second,
        owner_dev[:, :, 0], slot_row,
    )
    return (grad_up[None], grad_down[None], row_grad[None])


def solution(mesh):
    placed = (
        P("dp", "token", None),
        P("dp", "token", None),
        P("token", None, None),
        P("token", None, None),
        P("token", None),
        P("token", None),
        P("token", "dp", None),
        P("token", "dp"),
    )
    small = mesh.shape["dp"] == 4
    return jax.shard_map(
        small_group if small else per_device,
        mesh=mesh,
        in_specs=placed,
        out_specs=(P("token", "dp", None), P("token", "dp", None), P("token", "dp", None)),
        check_vma=False,
    )
```

```python
import functools

import jax
import jax.numpy as jnp
from jax import lax
from jax.experimental import pallas as pl
from jax.experimental.pallas import tpu as pltpu

from jax.sharding import PartitionSpec as P

HOT = 256


EPS = 1e-05
HALF_ROOT = 0.7071067811865476
INV_ROOT_TAU = 0.3989422804014327


def normalize(values):
    center = values - jnp.mean(values, axis=-1, keepdims=True)
    inv_scale = lax.rsqrt(jnp.mean(center * center, axis=-1, keepdims=True) + EPS)
    return (center * inv_scale, inv_scale)


def norm_back(grad_norm, normed, inv_scale):
    mean_grad = jnp.mean(grad_norm, axis=-1, keepdims=True)
    mean_proj = jnp.mean(grad_norm * normed, axis=-1, keepdims=True)
    return inv_scale * (grad_norm - mean_grad - normed * mean_proj)


def gelu_parts(pre_act):
    cumul = 0.5 * (1.0 + jax.scipy.special.erf(pre_act * HALF_ROOT))
    density = jnp.exp(-0.5 * pre_act * pre_act) * INV_ROOT_TAU
    return (pre_act * cumul, cumul + pre_act * density)


def contract_rows(left, right):
    return lax.dot_general(
        left, right, (((0,), (0,)), ((), ())), preferred_element_type=jnp.float32
    )


def contract_cols(left, right):
    return lax.dot_general(
        left, right, (((1,), (1,)), ((), ())), preferred_element_type=jnp.float32
    )


def per_device(mix_input, out_grad, w_up, w_down, gain_first, gain_second, owner_dev, slot_row):
    batch_rows = mix_input.shape[0]
    width = mix_input.shape[2]
    owners = lax.axis_size("dp")
    normed, inv_scale = normalize(mix_input[:, 0, :].astype(jnp.float32))
    hidden_in = (normed * gain_first[0]).astype(jnp.bfloat16)
    pre_act = jnp.dot(hidden_in, w_up[0], preferred_element_type=jnp.float32)
    act_value, act_slope = gelu_parts(pre_act)
    active = act_value.astype(jnp.bfloat16)
    outer_sum = jnp.dot(active, w_down[0], preferred_element_type=jnp.float32) + hidden_in.astype(
        jnp.float32
    )
    normed_out, inv_out = normalize(outer_sum)
    grad_wide = norm_back(
        out_grad[:, 0, :].astype(jnp.float32) * gain_second[0], normed_out, inv_out
    )
    grad_mid = grad_wide.astype(jnp.bfloat16)
    grad_act = contract_cols(grad_mid, w_down[0])
    grad_pre = (grad_act * act_slope).astype(jnp.bfloat16)
    up_whole = contract_rows(hidden_in, grad_pre)
    down_whole = contract_rows(active, grad_mid)
    grad_up, grad_down = (
        lax.psum_scatter(
            up_whole.astype(jnp.bfloat16), "dp", scatter_dimension=0, tiled=True
        ).astype(jnp.float32),
        lax.psum_scatter(
            down_whole.astype(jnp.bfloat16), "dp", scatter_dimension=0, tiled=True
        ).astype(jnp.float32),
    )
    grad_hidden = contract_cols(grad_pre, w_up[0]) + grad_wide
    grad_sum = norm_back(grad_hidden * gain_first[0], normed, inv_scale).astype(jnp.bfloat16)
    pieces = lax.axis_size("token")
    swapped = lax.all_to_all(
        grad_sum.reshape(batch_rows, pieces, width // pieces),
        "token",
        split_axis=1,
        concat_axis=1,
        tiled=True,
    )
    embed_grad = (
        grad_sum.astype(jnp.float32) + swapped.reshape(batch_rows, width).astype(jnp.float32)
    ).astype(jnp.bfloat16)
    owner_ids = owner_dev[0, :, 0]
    slot_ids = slot_row[0]
    capacity = max(2, 8 * (5 * batch_rows // (16 * owners)))
    owner_hot = (
        owner_ids[:, None] == lax.broadcasted_iota(jnp.int32, (batch_rows, owners), 1)
    ).astype(jnp.int32)
    rank_within = jnp.sum((jnp.cumsum(owner_hot, axis=0) - 1) * owner_hot, axis=1)
    place = owner_ids * capacity + rank_within
    dispatch_mask = (
        lax.broadcasted_iota(jnp.int32, (owners * capacity, batch_rows), 0) == place[None, :]
    )
    send_grad = jnp.dot(
        dispatch_mask.astype(jnp.bfloat16), embed_grad, preferred_element_type=jnp.float32
    )
    send_grad = send_grad.astype(jnp.bfloat16).reshape(owners, capacity, width)
    send_slot = jnp.sum(dispatch_mask.astype(jnp.int32) * (slot_ids + 1)[None, :], axis=1) - 1
    send_slot = send_slot.astype(jnp.float32).astype(jnp.bfloat16).reshape(owners, capacity)
    recv_grad, recv_slot = (
        lax.all_to_all(send_grad, "dp", split_axis=0, concat_axis=0, tiled=True),
        lax.all_to_all(send_slot, "dp", split_axis=0, concat_axis=0, tiled=True),
    )
    slot_values = recv_slot.reshape(1, owners * capacity).astype(jnp.float32)
    gather_hot = (
        lax.broadcasted_iota(jnp.int32, (HOT, owners * capacity), 0).astype(jnp.float32)
        == slot_values
    ).astype(jnp.bfloat16)
    row_grad = jnp.dot(
        gather_hot, recv_grad.reshape(owners * capacity, width), preferred_element_type=jnp.float32
    )
    return (grad_up[None], grad_down[None], row_grad[None])


SUB = 256
VMEM_BYTES = 56 * 1024 * 1024
MESH = pl.DeviceIdType.MESH


def contract_flat(left, right):
    return jnp.dot(left, right, preferred_element_type=jnp.float32)


def fused_kernel(
    n_tok,
    mix_in, grad_in, up_in, down_in, gain1_in, gain2_in, owner_in, slot_in,
    gup_v, gdown_v, mine_v,
    mix_v, mid_v, h_v, up_v, down_v, slope_v, act_v, hsel_v, wide_v, acc_v, grad_v,
    sum_v, swap_v, embed_v, far_v, part_v, back_v, gain1_v, gain2_v, owner_v, slot_v,
    up_sem, down_sem, load_sem, send_sem, recv_sem, swap_send, swap_recv,
):
    rows, width = grad_v.shape
    chunks, _, part = up_v.shape
    piece = width // n_tok
    half_w = width // 2
    half_r = rows // 2
    hot_rows = mine_v.shape[0]
    bf, f32 = jnp.bfloat16, jnp.float32
    me = lax.axis_index("dp")
    tok = lax.axis_index("token")
    col = lax.rem(me, 2)
    over_x = {"dp": me + 1 - 2 * col}
    over_y = {"dp": lax.rem(me + 2, 4)}

    def group(g):
        return pl.ds(g * rows, rows)

    def chunk_at(j):
        return lax.rem(j + me + 1, chunks)

    def remote(i, src, dst, device):
        return pltpu.make_async_remote_copy(
            src_ref=src, dst_ref=dst, send_sem=send_sem.at[i], recv_sem=recv_sem.at[i],
            device_id=device, device_id_type=MESH,
        )

    def load_up(j):
        c = chunk_at(j)
        cols = pl.ds(pl.multiple_of(c * part, part), part)
        return pltpu.make_async_copy(up_in.at[:, cols], up_v.at[c], up_sem.at[j])

    def load_down(j):
        c = chunk_at(j)
        lines = pl.ds(pl.multiple_of(c * part, part), part)
        return pltpu.make_async_copy(down_in.at[lines, :], down_v.at[c], down_sem.at[j])

    small = [
        (mix_in, mix_v.at[group(0)]),
        (gain1_in, gain1_v),
        (gain2_in, gain2_v),
        (grad_in, grad_v),
        (owner_in, owner_v.at[0]),
        (slot_in, slot_v.at[0]),
    ]
    loads = [pltpu.make_async_copy(s, d, load_sem.at[i]) for i, (s, d) in enumerate(small)]
    loads[0].start()
    loads[1].start()
    for j in range(chunks):
        load_up(j).start()
        load_down(j).start()
    for load in loads[2:]:
        load.start()

    barrier = pltpu.get_barrier_semaphore()
    for device in (over_x, over_y):
        pl.semaphore_signal(barrier, inc=1, device_id=device, device_id_type=MESH)
    for k in range(1, n_tok):
        peer = {"token": lax.rem(tok + k, n_tok)}
        pl.semaphore_signal(barrier, inc=1, device_id=peer, device_id_type=MESH)
    pl.semaphore_wait(barrier, n_tok + 1)

    loads[0].wait()
    mix_x = remote(0, mix_v.at[group(0)], mix_v.at[group(1)], over_x)
    mix_y = remote(1, mix_v.at[group(0)], mix_v.at[group(2)], over_y)
    ids = [
        remote(2, owner_in, owner_v.at[1], over_x),
        remote(3, slot_in, slot_v.at[1], over_x),
        remote(4, owner_in, owner_v.at[2], over_y),
        remote(5, slot_in, slot_v.at[2], over_y),
    ]
    for copy in [mix_x, mix_y] + ids:
        copy.start()

    def norm_group(g):
        normed, _ = normalize(mix_v[group(g), :].astype(f32))
        h_v[group(g), :] = (normed * gain1_v[...]).astype(bf)

    def pick_group(g):
        shape = (hsel_v.shape[0], width)
        row = lax.broadcasted_iota(jnp.int32, shape, 0) + me * shape[0]
        pick = (row == lax.broadcasted_iota(jnp.int32, shape, 1)).astype(bf)
        hsel_v[:, group(g)] = contract_cols(pick, h_v[group(g), :]).astype(bf)

    def activate(g, c):
        pres = [
            contract_flat(h_v[group(g), :], up_v[c, :, s : s + SUB]) for s in range(0, part, SUB)
        ]
        total = None
        for i, pre in enumerate(pres):
            cols = slice(i * SUB, (i + 1) * SUB)
            value, slope = gelu_parts(pre)
            act = value.astype(bf)
            act_v[group(g), cols] = act
            slope_v[c, group(g), cols] = slope.astype(bf)
            if g == 0:
                more = contract_flat(act, down_v[c, cols, :])
                total = more if total is None else total + more
        return total

    loads[1].wait()
    norm_group(0)
    acc_v[...] = h_v[group(0), :].astype(f32)

    @pl.loop(0, chunks)
    def _(j):
        load_up(j).wait()
        load_down(j).wait()
        acc_v[...] += activate(0, chunk_at(j))

    for load in loads[2:]:
        load.wait()
    normed, inv = normalize(acc_v[...])
    wide = norm_back(grad_v[...].astype(f32) * gain2_v[...], normed, inv)
    wide_v[...] = wide
    mid_v[group(0), :] = wide.astype(bf)
    mid_x = remote(6, mid_v.at[group(0)], mid_v.at[group(1)], over_x)
    mid_y = remote(7, mid_v.at[group(0)], mid_v.at[group(2)], over_y)
    mid_x.start()
    mid_y.start()

    def slope_group(g, c):
        grad_act = contract_cols(mid_v[group(g), :], down_v[c])
        grad_pre = (grad_act * slope_v[c, group(g), :].astype(f32)).astype(bf)
        slope_v[c, group(g), :] = grad_pre
        return grad_pre

    acc_v[...] = wide_v[...]

    @pl.loop(0, chunks)
    def _(c):
        acc_v[...] += contract_cols(slope_group(0, c), up_v[c])

    normed, inv = normalize(mix_v[group(0), :].astype(f32))
    grad_sum = norm_back(acc_v[...] * gain1_v[...], normed, inv)
    sum_v[...] = grad_sum.T.astype(bf)

    own_piece = pl.ds(pl.multiple_of(tok * piece, piece), piece)
    swaps = []
    for k in range(1, n_tok):
        peer = lax.rem(tok + k, n_tok)
        there = pl.ds(pl.multiple_of(peer * piece, piece), piece)
        swaps.append(
            pltpu.make_async_remote_copy(
                src_ref=sum_v.at[there], dst_ref=swap_v.at[own_piece],
                send_sem=swap_send.at[k - 1], recv_sem=swap_recv.at[k - 1],
                device_id={"token": peer}, device_id_type=MESH,
            )
        )
        swaps[-1].start()
    swap_v[own_piece, :] = sum_v[own_piece, :]

    first, second = pl.ds(0, half_r), pl.ds(half_r, half_r)

    def block(ref, g, part_of):
        return ref.at[pl.ds(g * rows + part_of * half_r, half_r)]

    mix_x.wait_recv()
    mix_dx = remote(8, block(mix_v, 1, 0), block(mix_v, 3, 0), over_y)
    mix_dx.start()
    mix_y.wait_recv()
    mix_dy = remote(9, block(mix_v, 2, 1), block(mix_v, 3, 1), over_x)
    mix_dy.start()

    def others(g):
        norm_group(g)
        pick_group(g)

        @pl.loop(0, chunks)
        def _(j):
            activate(g, chunk_at(j))

    pick_group(0)
    others(1)
    others(2)

    for copy in swaps:
        copy.wait_recv()
    embed_v[...] = (sum_v[...].astype(f32) + swap_v[...].astype(f32)).astype(bf)
    low, high = pl.ds(0, half_w), pl.ds(half_w, half_w)
    far_x = remote(10, embed_v.at[low], far_v.at[0], over_x)
    far_y = remote(11, embed_v.at[high], far_v.at[1], over_y)
    far_x.start()
    far_y.start()

    mid_x.wait_recv()
    mid_dx = remote(12, block(mid_v, 1, 0), block(mid_v, 3, 0), over_y)
    mid_dx.start()
    mid_y.wait_recv()
    mid_dy = remote(13, block(mid_v, 2, 1), block(mid_v, 3, 1), over_x)
    mid_dy.start()

    pair = pl.ds(0, 2 * rows)

    @pl.loop(0, chunks)
    def _(c):
        slope_group(1, c)
        gup_v[c] = contract_flat(hsel_v[:, pair], slope_v[c, pair, :])

    gdown_v[...] = contract_rows(act_v[pair, :], mid_v[pair, :])

    @pl.loop(0, chunks)
    def _(c):
        grad_pre = slope_group(2, c)
        gup_v[c] += contract_flat(hsel_v[:, group(2)], grad_pre)

    gdown_v[...] += contract_rows(act_v[group(2), :], mid_v[group(2), :])

    mix_dx.wait_recv()
    mix_dy.wait_recv()
    others(3)

    for copy in ids:
        copy.wait_recv()
    far_x.wait_recv()
    far_y.wait_recv()

    def hot(k, owner):
        target = owner_v[k] * hot_rows + slot_v[k]
        row = lax.broadcasted_iota(jnp.int32, (hot_rows, rows), 0) + owner * hot_rows
        return (row == target).astype(bf)

    def merge(owner, k, cols):
        kept = contract_cols(hot(0, owner), embed_v[cols, :])
        return kept + contract_cols(hot(k, owner), far_v[k - 1])

    part_v[0] = merge(over_y["dp"], 1, low).astype(bf)
    part_v[1] = merge(over_x["dp"], 2, high).astype(bf)
    back_y = remote(14, part_v.at[0], back_v.at[0], over_y)
    back_x = remote(15, part_v.at[1], back_v.at[1], over_x)
    back_y.start()
    back_x.start()
    mine_v[:, :half_w] = merge(me, 1, low)
    mine_v[:, half_w:] = merge(me, 2, high)

    mid_dx.wait_recv()
    mid_dy.wait_recv()

    @pl.loop(0, chunks)
    def _(c):
        grad_pre = slope_group(3, c)
        gup_v[c] += contract_flat(hsel_v[:, group(3)], grad_pre)

    gdown_v[...] += contract_rows(act_v[group(3), :], mid_v[group(3), :])

    back_y.wait_recv()
    back_x.wait_recv()
    mine_v[:, :half_w] += back_v[0].astype(f32)
    mine_v[:, half_w:] += back_v[1].astype(f32)

    for copy in [mix_x, mix_y] + ids + [mid_x, mid_y, mix_dx, mix_dy] + swaps:
        copy.wait_send()
    for copy in [far_x, far_y, mid_dx, mid_dy, back_x, back_y]:
        copy.wait_send()


def store_kernel(up_ref, down_ref, rows_ref, up_out, down_out, rows_out, sems):
    chunks, _, part = up_ref.shape
    copies = [
        pltpu.make_async_copy(up_ref.at[c], up_out.at[:, pl.ds(c * part, part)], sems.at[c])
        for c in range(chunks)
    ]
    quarter = part // chunks
    for c in range(chunks):
        lines = pl.ds(c * quarter, quarter)
        copies.append(
            pltpu.make_async_copy(down_ref.at[lines], down_out.at[lines], sems.at[chunks + c])
        )
    copies.append(pltpu.make_async_copy(rows_ref, rows_out, sems.at[2 * chunks]))
    for copy in copies:
        copy.start()
    for copy in copies:
        copy.wait()


def small_group(mix_input, out_grad, w_up, w_down, gain_first, gain_second, owner_dev, slot_row):
    rows = mix_input.shape[0]
    width = mix_input.shape[2]
    hidden = w_up.shape[2]
    groups = lax.axis_size("dp")
    n_tok = lax.axis_size("token")
    part = hidden // groups
    own = width // groups
    half = width // 2
    bf, f32, i32 = jnp.bfloat16, jnp.float32, jnp.int32
    vm, dma = pltpu.VMEM, pltpu.SemaphoreType.DMA
    main = pl.BlockSpec(memory_space=pltpu.HBM)
    inside = pl.BlockSpec(memory_space=pltpu.VMEM)
    unit = 2 * rows * width * hidden
    held = pl.pallas_call(
        functools.partial(fused_kernel, n_tok),
        in_specs=[main] * 8,
        out_specs=[inside] * 3,
        out_shape=[vm((groups, own, part), f32), vm((part, width), f32), vm((HOT, width), f32)],
        scratch_shapes=[
            vm((groups * rows, width), bf),
            vm((groups * rows, width), bf),
            vm((groups * rows, width), bf),
            vm((groups, width, part), bf),
            vm((groups, part, width), bf),
            vm((groups, groups * rows, part), bf),
            vm((groups * rows, part), bf),
            vm((own, groups * rows), bf),
            vm((rows, width), f32),
            vm((rows, width), f32),
            vm((rows, width), bf),
            vm((width, rows), bf),
            vm((width, rows), bf),
            vm((width, rows), bf),
            vm((2, half, rows), bf),
            vm((2, HOT, half), bf),
            vm((2, HOT, half), bf),
            vm((1, width), f32),
            vm((1, width), f32),
            vm((3, 1, rows), i32),
            vm((3, 1, rows), i32),
            dma((groups,)),
            dma((groups,)),
            dma((6,)),
            dma((16,)),
            dma((16,)),
            dma((n_tok - 1,)),
            dma((n_tok - 1,)),
        ],
        compiler_params=pltpu.CompilerParams(
            vmem_limit_bytes=VMEM_BYTES, collective_id=0, has_side_effects=True
        ),
        cost_estimate=pl.CostEstimate(
            flops=12 * unit, bytes_accessed=8 * width * hidden, transcendentals=0
        ),
        name="fused",
    )(
        mix_input[:, 0, :], out_grad[:, 0, :], w_up[0], w_down[0], gain_first, gain_second,
        owner_dev[:, :, 0], slot_row,
    )
    grad_up, grad_down, row_grad = pl.pallas_call(
        store_kernel,
        in_specs=[pl.BlockSpec(memory_space=pl.ANY)] * 3,
        out_specs=[main] * 3,
        out_shape=[
            jax.ShapeDtypeStruct((own, hidden), f32),
            jax.ShapeDtypeStruct((part, width), f32),
            jax.ShapeDtypeStruct((HOT, width), f32),
        ],
        scratch_shapes=[dma((2 * groups + 1,))],
        compiler_params=pltpu.CompilerParams(vmem_limit_bytes=1 << 20),
        name="store",
    )(*held)
    return (grad_up[None], grad_down[None], row_grad[None])


def solution(mesh):
    placed = (
        P("dp", "token", None),
        P("dp", "token", None),
        P("token", None, None),
        P("token", None, None),
        P("token", None),
        P("token", None),
        P("token", "dp", None),
        P("token", "dp"),
    )
    small = mesh.shape["dp"] == 4
    return jax.shard_map(
        small_group if small else per_device,
        mesh=mesh,
        in_specs=placed,
        out_specs=(P("token", "dp", None), P("token", "dp", None), P("token", "dp", None)),
        check_vma=False,
    )
```

```python
import functools

import jax
import jax.numpy as jnp
from jax import lax
from jax.experimental import pallas as pl
from jax.experimental.pallas import tpu as pltpu

from jax.sharding import PartitionSpec as P

HOT = 256


EPS = 1e-05
HALF_ROOT = 0.7071067811865476
INV_ROOT_TAU = 0.3989422804014327


def normalize(values):
    center = values - jnp.mean(values, axis=-1, keepdims=True)
    inv_scale = lax.rsqrt(jnp.mean(center * center, axis=-1, keepdims=True) + EPS)
    return (center * inv_scale, inv_scale)


def norm_back(grad_norm, normed, inv_scale):
    mean_grad = jnp.mean(grad_norm, axis=-1, keepdims=True)
    mean_proj = jnp.mean(grad_norm * normed, axis=-1, keepdims=True)
    return inv_scale * (grad_norm - mean_grad - normed * mean_proj)


def gelu_parts(pre_act):
    cumul = 0.5 * (1.0 + jax.scipy.special.erf(pre_act * HALF_ROOT))
    density = jnp.exp(-0.5 * pre_act * pre_act) * INV_ROOT_TAU
    return (pre_act * cumul, cumul + pre_act * density)


def contract_rows(left, right):
    return lax.dot_general(
        left, right, (((0,), (0,)), ((), ())), preferred_element_type=jnp.float32
    )


def contract_cols(left, right):
    return lax.dot_general(
        left, right, (((1,), (1,)), ((), ())), preferred_element_type=jnp.float32
    )


def per_device(mix_input, out_grad, w_up, w_down, gain_first, gain_second, owner_dev, slot_row):
    batch_rows = mix_input.shape[0]
    width = mix_input.shape[2]
    owners = lax.axis_size("dp")
    normed, inv_scale = normalize(mix_input[:, 0, :].astype(jnp.float32))
    hidden_in = (normed * gain_first[0]).astype(jnp.bfloat16)
    pre_act = jnp.dot(hidden_in, w_up[0], preferred_element_type=jnp.float32)
    act_value, act_slope = gelu_parts(pre_act)
    active = act_value.astype(jnp.bfloat16)
    outer_sum = jnp.dot(active, w_down[0], preferred_element_type=jnp.float32) + hidden_in.astype(
        jnp.float32
    )
    normed_out, inv_out = normalize(outer_sum)
    grad_wide = norm_back(
        out_grad[:, 0, :].astype(jnp.float32) * gain_second[0], normed_out, inv_out
    )
    grad_mid = grad_wide.astype(jnp.bfloat16)
    grad_act = contract_cols(grad_mid, w_down[0])
    grad_pre = (grad_act * act_slope).astype(jnp.bfloat16)
    up_whole = contract_rows(hidden_in, grad_pre)
    down_whole = contract_rows(active, grad_mid)
    grad_up, grad_down = (
        lax.psum_scatter(
            up_whole.astype(jnp.bfloat16), "dp", scatter_dimension=0, tiled=True
        ).astype(jnp.float32),
        lax.psum_scatter(
            down_whole.astype(jnp.bfloat16), "dp", scatter_dimension=0, tiled=True
        ).astype(jnp.float32),
    )
    grad_hidden = contract_cols(grad_pre, w_up[0]) + grad_wide
    grad_sum = norm_back(grad_hidden * gain_first[0], normed, inv_scale).astype(jnp.bfloat16)
    pieces = lax.axis_size("token")
    swapped = lax.all_to_all(
        grad_sum.reshape(batch_rows, pieces, width // pieces),
        "token",
        split_axis=1,
        concat_axis=1,
        tiled=True,
    )
    embed_grad = (
        grad_sum.astype(jnp.float32) + swapped.reshape(batch_rows, width).astype(jnp.float32)
    ).astype(jnp.bfloat16)
    owner_ids = owner_dev[0, :, 0]
    slot_ids = slot_row[0]
    capacity = max(2, 8 * (5 * batch_rows // (16 * owners)))
    owner_hot = (
        owner_ids[:, None] == lax.broadcasted_iota(jnp.int32, (batch_rows, owners), 1)
    ).astype(jnp.int32)
    rank_within = jnp.sum((jnp.cumsum(owner_hot, axis=0) - 1) * owner_hot, axis=1)
    place = owner_ids * capacity + rank_within
    dispatch_mask = (
        lax.broadcasted_iota(jnp.int32, (owners * capacity, batch_rows), 0) == place[None, :]
    )
    send_grad = jnp.dot(
        dispatch_mask.astype(jnp.bfloat16), embed_grad, preferred_element_type=jnp.float32
    )
    send_grad = send_grad.astype(jnp.bfloat16).reshape(owners, capacity, width)
    send_slot = jnp.sum(dispatch_mask.astype(jnp.int32) * (slot_ids + 1)[None, :], axis=1) - 1
    send_slot = send_slot.astype(jnp.float32).astype(jnp.bfloat16).reshape(owners, capacity)
    recv_grad, recv_slot = (
        lax.all_to_all(send_grad, "dp", split_axis=0, concat_axis=0, tiled=True),
        lax.all_to_all(send_slot, "dp", split_axis=0, concat_axis=0, tiled=True),
    )
    slot_values = recv_slot.reshape(1, owners * capacity).astype(jnp.float32)
    gather_hot = (
        lax.broadcasted_iota(jnp.int32, (HOT, owners * capacity), 0).astype(jnp.float32)
        == slot_values
    ).astype(jnp.bfloat16)
    row_grad = jnp.dot(
        gather_hot, recv_grad.reshape(owners * capacity, width), preferred_element_type=jnp.float32
    )
    return (grad_up[None], grad_down[None], row_grad[None])


SUB = 256
UNROLL = 4
VMEM_BYTES = 56 * 1024 * 1024
MESH = pl.DeviceIdType.MESH


def contract_flat(left, right):
    return jnp.dot(left, right, preferred_element_type=jnp.float32)


def fused_kernel(
    n_tok,
    mix_in, grad_in, up_in, down_in, gain1_in, gain2_in, owner_in, slot_in,
    gup_v, gdown_v, mine_v,
    mix_v, mid_v, h_v, up_v, down_v, slope_v, act_v, hsel_v, wide_v, acc_v, grad_v,
    sum_v, swap_v, embed_v, far_v, part_v, back_v, gain1_v, gain2_v, owner_v, slot_v,
    up_sem, down_sem, load_sem, send_sem, recv_sem, swap_send, swap_recv, ready_sem, go_sem,
):
    rows, width = grad_v.shape
    chunks, _, part = up_v.shape
    piece = width // n_tok
    half_w = width // 2
    half_r = rows // 2
    hot_rows = mine_v.shape[0]
    bf, f32 = jnp.bfloat16, jnp.float32
    me = lax.axis_index("dp")
    tok = lax.axis_index("token")
    col = lax.rem(me, 2)
    over_x = {"dp": me + 1 - 2 * col}
    over_y = {"dp": lax.rem(me + 2, 4)}

    def group(g):
        return pl.ds(g * rows, rows)

    def chunk_at(j):
        return lax.rem(j + me + 1, chunks)

    def remote(i, src, dst, device):
        return pltpu.make_async_remote_copy(
            src_ref=src, dst_ref=dst, send_sem=send_sem.at[i], recv_sem=recv_sem.at[i],
            device_id=device, device_id_type=MESH,
        )

    def load_up(j):
        c = chunk_at(j)
        cols = pl.ds(pl.multiple_of(c * part, part), part)
        return pltpu.make_async_copy(up_in.at[:, cols], up_v.at[c], up_sem.at[j])

    def load_down(j):
        c = chunk_at(j)
        lines = pl.ds(pl.multiple_of(c * part, part), part)
        return pltpu.make_async_copy(down_in.at[lines, :], down_v.at[c], down_sem.at[j])

    small = [
        (mix_in, mix_v.at[group(0)]),
        (gain1_in, gain1_v),
        (gain2_in, gain2_v),
        (grad_in, grad_v),
        (owner_in, owner_v.at[0]),
        (slot_in, slot_v.at[0]),
    ]
    loads = [pltpu.make_async_copy(s, d, load_sem.at[i]) for i, (s, d) in enumerate(small)]
    loads[0].start()
    loads[1].start()
    for j in range(chunks):
        load_up(j).start()
        load_down(j).start()
    for load in loads[2:]:
        load.start()

    barrier = pltpu.get_barrier_semaphore()
    for device in (over_x, over_y):
        pl.semaphore_signal(barrier, inc=1, device_id=device, device_id_type=MESH)

    @pl.when(tok == 0)
    def _():
        for k in range(1, n_tok):
            pl.semaphore_signal(barrier, inc=1, device_id={"token": k}, device_id_type=MESH)
        pl.semaphore_wait(barrier, 2)

    @pl.when(tok != 0)
    def _():
        pl.semaphore_wait(barrier, 3)
        pl.semaphore_signal(ready_sem, inc=1, device_id={"token": 0}, device_id_type=MESH)

    loads[0].wait()
    mix_x = remote(0, mix_v.at[group(0)], mix_v.at[group(1)], over_x)
    mix_y = remote(1, mix_v.at[group(0)], mix_v.at[group(2)], over_y)
    ids = [
        remote(2, owner_in, owner_v.at[1], over_x),
        remote(3, slot_in, slot_v.at[1], over_x),
        remote(4, owner_in, owner_v.at[2], over_y),
        remote(5, slot_in, slot_v.at[2], over_y),
    ]
    for copy in [mix_x, mix_y] + ids:
        copy.start()

    def norm_group(g):
        normed, _ = normalize(mix_v[group(g), :].astype(f32))
        h_v[group(g), :] = (normed * gain1_v[...]).astype(bf)

    def pick_group(g):
        shape = (hsel_v.shape[0], width)
        row = lax.broadcasted_iota(jnp.int32, shape, 0) + me * shape[0]
        pick = (row == lax.broadcasted_iota(jnp.int32, shape, 1)).astype(bf)
        hsel_v[:, group(g)] = contract_cols(pick, h_v[group(g), :]).astype(bf)

    def activate(g, c):
        pres = [
            contract_flat(h_v[group(g), :], up_v[c, :, s : s + SUB]) for s in range(0, part, SUB)
        ]
        total = None
        for i, pre in enumerate(pres):
            cols = slice(i * SUB, (i + 1) * SUB)
            value, slope = gelu_parts(pre)
            act = value.astype(bf)
            act_v[group(g), cols] = act
            slope_v[c, group(g), cols] = slope.astype(bf)
            if g == 0:
                more = contract_flat(act, down_v[c, cols, :])
                total = more if total is None else total + more
        return total

    loads[1].wait()
    norm_group(0)
    acc_v[...] = h_v[group(0), :].astype(f32)

    @pl.loop(0, chunks, unroll=UNROLL)
    def _(j):
        load_up(j).wait()
        load_down(j).wait()
        acc_v[...] += activate(0, chunk_at(j))

    for load in loads[2:]:
        load.wait()
    normed, inv = normalize(acc_v[...])
    wide = norm_back(grad_v[...].astype(f32) * gain2_v[...], normed, inv)
    wide_v[...] = wide
    mid_v[group(0), :] = wide.astype(bf)
    mid_x = remote(6, mid_v.at[group(0)], mid_v.at[group(1)], over_x)
    mid_y = remote(7, mid_v.at[group(0)], mid_v.at[group(2)], over_y)
    mid_x.start()
    mid_y.start()

    @pl.when(tok == 0)
    def _():
        pl.semaphore_wait(ready_sem, n_tok - 1)
        for k in range(1, n_tok):
            pl.semaphore_signal(go_sem, inc=1, device_id={"token": k}, device_id_type=MESH)

    def slope_group(g, c):
        grad_act = contract_cols(mid_v[group(g), :], down_v[c])
        grad_pre = (grad_act * slope_v[c, group(g), :].astype(f32)).astype(bf)
        slope_v[c, group(g), :] = grad_pre
        return grad_pre

    acc_v[...] = wide_v[...]

    @pl.loop(0, chunks, unroll=UNROLL)
    def _(c):
        acc_v[...] += contract_cols(slope_group(0, c), up_v[c])

    normed, inv = normalize(mix_v[group(0), :].astype(f32))
    grad_sum = norm_back(acc_v[...] * gain1_v[...], normed, inv)
    sum_v[...] = grad_sum.T.astype(bf)

    @pl.when(tok != 0)
    def _():
        pl.semaphore_wait(go_sem, 1)

    own_piece = pl.ds(pl.multiple_of(tok * piece, piece), piece)
    swaps = []
    for k in range(1, n_tok):
        peer = lax.rem(tok + k, n_tok)
        there = pl.ds(pl.multiple_of(peer * piece, piece), piece)
        swaps.append(
            pltpu.make_async_remote_copy(
                src_ref=sum_v.at[there], dst_ref=swap_v.at[own_piece],
                send_sem=swap_send.at[k - 1], recv_sem=swap_recv.at[k - 1],
                device_id={"token": peer}, device_id_type=MESH,
            )
        )
        swaps[-1].start()
    swap_v[own_piece, :] = sum_v[own_piece, :]

    first, second = pl.ds(0, half_r), pl.ds(half_r, half_r)

    def block(ref, g, part_of):
        return ref.at[pl.ds(g * rows + part_of * half_r, half_r)]

    mix_x.wait_recv()
    mix_dx = remote(8, block(mix_v, 1, 0), block(mix_v, 3, 0), over_y)
    mix_dx.start()
    mix_y.wait_recv()
    mix_dy = remote(9, block(mix_v, 2, 1), block(mix_v, 3, 1), over_x)
    mix_dy.start()

    def others(g):
        norm_group(g)
        pick_group(g)

        @pl.loop(0, chunks, unroll=UNROLL)
        def _(j):
            activate(g, chunk_at(j))

    pick_group(0)
    others(1)
    others(2)

    def piece_of(g, k):
        return mid_v.at[pl.ds(g * rows + k * (half_r // 2), half_r // 2)]

    mid_x.wait_recv()
    mid_y.wait_recv()
    mid_d = [
        remote(12, piece_of(1, 0), piece_of(3, 0), over_y),
        remote(13, piece_of(2, 2), piece_of(3, 2), over_x),
        remote(16, piece_of(1, 1), piece_of(3, 1), over_y),
        remote(17, piece_of(2, 3), piece_of(3, 3), over_x),
    ]
    mid_d[0].start()
    mid_d[1].start()

    pair = pl.ds(0, 2 * rows)

    @pl.loop(0, chunks, unroll=UNROLL)
    def _(c):
        slope_group(1, c)
        gup_v[c] = contract_flat(hsel_v[:, pair], slope_v[c, pair, :])

    for copy in swaps:
        copy.wait_recv()
    embed_v[...] = (sum_v[...].astype(f32) + swap_v[...].astype(f32)).astype(bf)
    low, high = pl.ds(0, half_w), pl.ds(half_w, half_w)
    far_x = remote(10, embed_v.at[low], far_v.at[0], over_x)
    far_y = remote(11, embed_v.at[high], far_v.at[1], over_y)
    far_x.start()
    far_y.start()
    mid_d[2].start()
    mid_d[3].start()

    gdown_v[...] = contract_rows(act_v[pair, :], mid_v[pair, :])

    @pl.loop(0, chunks, unroll=UNROLL)
    def _(c):
        grad_pre = slope_group(2, c)
        gup_v[c] += contract_flat(hsel_v[:, group(2)], grad_pre)

    gdown_v[...] += contract_rows(act_v[group(2), :], mid_v[group(2), :])

    mix_dx.wait_recv()
    mix_dy.wait_recv()
    others(3)

    for copy in ids:
        copy.wait_recv()
    far_x.wait_recv()
    far_y.wait_recv()

    def hot(k, owner):
        target = owner_v[k] * hot_rows + slot_v[k]
        row = lax.broadcasted_iota(jnp.int32, (hot_rows, rows), 0) + owner * hot_rows
        return (row == target).astype(bf)

    def merge(owner, k, cols):
        kept = contract_cols(hot(0, owner), embed_v[cols, :])
        return kept + contract_cols(hot(k, owner), far_v[k - 1])

    part_v[0] = merge(over_y["dp"], 1, low).astype(bf)
    part_v[1] = merge(over_x["dp"], 2, high).astype(bf)
    back_y = remote(14, part_v.at[0], back_v.at[0], over_y)
    back_x = remote(15, part_v.at[1], back_v.at[1], over_x)
    back_y.start()
    back_x.start()
    mine_v[:, :half_w] = merge(me, 1, low)
    mine_v[:, half_w:] = merge(me, 2, high)

    for copy in mid_d:
        copy.wait_recv()

    @pl.loop(0, chunks, unroll=UNROLL)
    def _(c):
        grad_pre = slope_group(3, c)
        gup_v[c] += contract_flat(hsel_v[:, group(3)], grad_pre)

    gdown_v[...] += contract_rows(act_v[group(3), :], mid_v[group(3), :])

    back_y.wait_recv()
    back_x.wait_recv()
    mine_v[:, :half_w] += back_v[0].astype(f32)
    mine_v[:, half_w:] += back_v[1].astype(f32)

    for copy in [mix_x, mix_y] + ids + [mid_x, mid_y, mix_dx, mix_dy] + swaps:
        copy.wait_send()
    for copy in [far_x, far_y, back_x, back_y] + mid_d:
        copy.wait_send()


def store_kernel(up_ref, down_ref, rows_ref, up_out, down_out, rows_out, sems):
    chunks, _, part = up_ref.shape
    copies = [
        pltpu.make_async_copy(up_ref.at[c], up_out.at[:, pl.ds(c * part, part)], sems.at[c])
        for c in range(chunks)
    ]
    quarter = part // chunks
    for c in range(chunks):
        lines = pl.ds(c * quarter, quarter)
        copies.append(
            pltpu.make_async_copy(down_ref.at[lines], down_out.at[lines], sems.at[chunks + c])
        )
    copies.append(pltpu.make_async_copy(rows_ref, rows_out, sems.at[2 * chunks]))
    for copy in copies:
        copy.start()
    for copy in copies:
        copy.wait()


def small_group(mix_input, out_grad, w_up, w_down, gain_first, gain_second, owner_dev, slot_row):
    rows = mix_input.shape[0]
    width = mix_input.shape[2]
    hidden = w_up.shape[2]
    groups = lax.axis_size("dp")
    n_tok = lax.axis_size("token")
    part = hidden // groups
    own = width // groups
    half = width // 2
    bf, f32, i32 = jnp.bfloat16, jnp.float32, jnp.int32
    vm, dma = pltpu.VMEM, pltpu.SemaphoreType.DMA
    main = pl.BlockSpec(memory_space=pltpu.HBM)
    inside = pl.BlockSpec(memory_space=pltpu.VMEM)
    unit = 2 * rows * width * hidden
    held = pl.pallas_call(
        functools.partial(fused_kernel, n_tok),
        in_specs=[main] * 8,
        out_specs=[inside] * 3,
        out_shape=[vm((groups, own, part), f32), vm((part, width), f32), vm((HOT, width), f32)],
        scratch_shapes=[
            vm((groups * rows, width), bf),
            vm((groups * rows, width), bf),
            vm((groups * rows, width), bf),
            vm((groups, width, part), bf),
            vm((groups, part, width), bf),
            vm((groups, groups * rows, part), bf),
            vm((groups * rows, part), bf),
            vm((own, groups * rows), bf),
            vm((rows, width), f32),
            vm((rows, width), f32),
            vm((rows, width), bf),
            vm((width, rows), bf),
            vm((width, rows), bf),
            vm((width, rows), bf),
            vm((2, half, rows), bf),
            vm((2, HOT, half), bf),
            vm((2, HOT, half), bf),
            vm((1, width), f32),
            vm((1, width), f32),
            vm((3, 1, rows), i32),
            vm((3, 1, rows), i32),
            dma((groups,)),
            dma((groups,)),
            dma((6,)),
            dma((18,)),
            dma((18,)),
            dma((n_tok - 1,)),
            dma((n_tok - 1,)),
            pltpu.SemaphoreType.REGULAR,
            pltpu.SemaphoreType.REGULAR,
        ],
        compiler_params=pltpu.CompilerParams(
            vmem_limit_bytes=VMEM_BYTES, collective_id=0, has_side_effects=True
        ),
        cost_estimate=pl.CostEstimate(
            flops=12 * unit, bytes_accessed=8 * width * hidden, transcendentals=0
        ),
        name="fused",
    )(
        mix_input[:, 0, :], out_grad[:, 0, :], w_up[0], w_down[0], gain_first, gain_second,
        owner_dev[:, :, 0], slot_row,
    )
    grad_up, grad_down, row_grad = pl.pallas_call(
        store_kernel,
        in_specs=[pl.BlockSpec(memory_space=pl.ANY)] * 3,
        out_specs=[main] * 3,
        out_shape=[
            jax.ShapeDtypeStruct((own, hidden), f32),
            jax.ShapeDtypeStruct((part, width), f32),
            jax.ShapeDtypeStruct((HOT, width), f32),
        ],
        scratch_shapes=[dma((2 * groups + 1,))],
        compiler_params=pltpu.CompilerParams(vmem_limit_bytes=1 << 20),
        name="store",
    )(*held)
    return (grad_up[None], grad_down[None], row_grad[None])


def solution(mesh):
    placed = (
        P("dp", "token", None),
        P("dp", "token", None),
        P("token", None, None),
        P("token", None, None),
        P("token", None),
        P("token", None),
        P("token", "dp", None),
        P("token", "dp"),
    )
    small = mesh.shape["dp"] == 4
    return jax.shard_map(
        small_group if small else per_device,
        mesh=mesh,
        in_specs=placed,
        out_specs=(P("token", "dp", None), P("token", "dp", None), P("token", "dp", None)),
        check_vma=False,
    )
```

```python
import functools

import jax
import jax.numpy as jnp
from jax import lax
from jax.experimental import pallas as pl
from jax.experimental.pallas import tpu as pltpu

from jax.sharding import PartitionSpec as P

HOT = 256


EPS = 1e-05
HALF_ROOT = 0.7071067811865476
INV_ROOT_TAU = 0.3989422804014327


def normalize(values):
    center = values - jnp.mean(values, axis=-1, keepdims=True)
    inv_scale = lax.rsqrt(jnp.mean(center * center, axis=-1, keepdims=True) + EPS)
    return (center * inv_scale, inv_scale)


def norm_back(grad_norm, normed, inv_scale):
    mean_grad = jnp.mean(grad_norm, axis=-1, keepdims=True)
    mean_proj = jnp.mean(grad_norm * normed, axis=-1, keepdims=True)
    return inv_scale * (grad_norm - mean_grad - normed * mean_proj)


def gelu_parts(pre_act):
    cumul = 0.5 * (1.0 + jax.scipy.special.erf(pre_act * HALF_ROOT))
    density = jnp.exp(-0.5 * pre_act * pre_act) * INV_ROOT_TAU
    return (pre_act * cumul, cumul + pre_act * density)


def contract_rows(left, right):
    return lax.dot_general(
        left, right, (((0,), (0,)), ((), ())), preferred_element_type=jnp.float32
    )


def contract_cols(left, right):
    return lax.dot_general(
        left, right, (((1,), (1,)), ((), ())), preferred_element_type=jnp.float32
    )


def per_device(mix_input, out_grad, w_up, w_down, gain_first, gain_second, owner_dev, slot_row):
    batch_rows = mix_input.shape[0]
    width = mix_input.shape[2]
    owners = lax.axis_size("dp")
    normed, inv_scale = normalize(mix_input[:, 0, :].astype(jnp.float32))
    hidden_in = (normed * gain_first[0]).astype(jnp.bfloat16)
    pre_act = jnp.dot(hidden_in, w_up[0], preferred_element_type=jnp.float32)
    act_value, act_slope = gelu_parts(pre_act)
    active = act_value.astype(jnp.bfloat16)
    outer_sum = jnp.dot(active, w_down[0], preferred_element_type=jnp.float32) + hidden_in.astype(
        jnp.float32
    )
    normed_out, inv_out = normalize(outer_sum)
    grad_wide = norm_back(
        out_grad[:, 0, :].astype(jnp.float32) * gain_second[0], normed_out, inv_out
    )
    grad_mid = grad_wide.astype(jnp.bfloat16)
    grad_act = contract_cols(grad_mid, w_down[0])
    grad_pre = (grad_act * act_slope).astype(jnp.bfloat16)
    up_whole = contract_rows(hidden_in, grad_pre)
    down_whole = contract_rows(active, grad_mid)
    grad_up, grad_down = (
        lax.psum_scatter(
            up_whole.astype(jnp.bfloat16), "dp", scatter_dimension=0, tiled=True
        ).astype(jnp.float32),
        lax.psum_scatter(
            down_whole.astype(jnp.bfloat16), "dp", scatter_dimension=0, tiled=True
        ).astype(jnp.float32),
    )
    grad_hidden = contract_cols(grad_pre, w_up[0]) + grad_wide
    grad_sum = norm_back(grad_hidden * gain_first[0], normed, inv_scale).astype(jnp.bfloat16)
    pieces = lax.axis_size("token")
    swapped = lax.all_to_all(
        grad_sum.reshape(batch_rows, pieces, width // pieces),
        "token",
        split_axis=1,
        concat_axis=1,
        tiled=True,
    )
    embed_grad = (
        grad_sum.astype(jnp.float32) + swapped.reshape(batch_rows, width).astype(jnp.float32)
    ).astype(jnp.bfloat16)
    owner_ids = owner_dev[0, :, 0]
    slot_ids = slot_row[0]
    capacity = max(2, 8 * (5 * batch_rows // (16 * owners)))
    owner_hot = (
        owner_ids[:, None] == lax.broadcasted_iota(jnp.int32, (batch_rows, owners), 1)
    ).astype(jnp.int32)
    rank_within = jnp.sum((jnp.cumsum(owner_hot, axis=0) - 1) * owner_hot, axis=1)
    place = owner_ids * capacity + rank_within
    dispatch_mask = (
        lax.broadcasted_iota(jnp.int32, (owners * capacity, batch_rows), 0) == place[None, :]
    )
    send_grad = jnp.dot(
        dispatch_mask.astype(jnp.bfloat16), embed_grad, preferred_element_type=jnp.float32
    )
    send_grad = send_grad.astype(jnp.bfloat16).reshape(owners, capacity, width)
    send_slot = jnp.sum(dispatch_mask.astype(jnp.int32) * (slot_ids + 1)[None, :], axis=1) - 1
    send_slot = send_slot.astype(jnp.float32).astype(jnp.bfloat16).reshape(owners, capacity)
    recv_grad, recv_slot = (
        lax.all_to_all(send_grad, "dp", split_axis=0, concat_axis=0, tiled=True),
        lax.all_to_all(send_slot, "dp", split_axis=0, concat_axis=0, tiled=True),
    )
    slot_values = recv_slot.reshape(1, owners * capacity).astype(jnp.float32)
    gather_hot = (
        lax.broadcasted_iota(jnp.int32, (HOT, owners * capacity), 0).astype(jnp.float32)
        == slot_values
    ).astype(jnp.bfloat16)
    row_grad = jnp.dot(
        gather_hot, recv_grad.reshape(owners * capacity, width), preferred_element_type=jnp.float32
    )
    return (grad_up[None], grad_down[None], row_grad[None])


SUB = 256
UNROLL = 4
VMEM_BYTES = 56 * 1024 * 1024
MESH = pl.DeviceIdType.MESH


def contract_flat(left, right):
    return jnp.dot(left, right, preferred_element_type=jnp.float32)


def fused_kernel(
    n_tok,
    mix_in, grad_in, up_in, down_in, gain1_in, gain2_in, owner_in, slot_in,
    gup_v, gdown_v, mine_v,
    mix_v, mid_v, h_v, up_v, down_v, slope_v, act_v, hsel_v, hlast_v, wide_v, acc_v, grad_v,
    sum_v, swap_v, embed_v, far_v, part_v, back_v, gain1_v, gain2_v, owner_v, slot_v,
    up_sem, down_sem, load_sem, send_sem, recv_sem, swap_send, swap_recv, ready_sem, go_sem, x_sem, y_sem,
):
    rows, width = grad_v.shape
    chunks, _, part = up_v.shape
    piece = width // n_tok
    half_w = width // 2
    half_r = rows // 2
    hot_rows = mine_v.shape[0]
    bf, f32 = jnp.bfloat16, jnp.float32
    me = lax.axis_index("dp")
    tok = lax.axis_index("token")
    col = lax.rem(me, 2)
    over_x = {"dp": me + 1 - 2 * col}
    row = me // 2
    over_y = {"dp": lax.rem(me + 2, 4)}

    barrier = pltpu.get_barrier_semaphore()

    @pl.when(col == 0)
    def _():
        pl.semaphore_signal(barrier, inc=1, device_id=over_x, device_id_type=MESH)

    @pl.when(row == 0)
    def _():
        pl.semaphore_signal(barrier, inc=1, device_id=over_y, device_id_type=MESH)

    @pl.when(tok == 0)
    def _():
        for k in range(1, n_tok):
            pl.semaphore_signal(barrier, inc=1, device_id={"token": k}, device_id_type=MESH)

    def group(g):
        return pl.ds(g * rows, rows)

    def chunk_at(j):
        return lax.rem(j + me + 1, chunks)

    def remote(i, src, dst, device):
        return pltpu.make_async_remote_copy(
            src_ref=src, dst_ref=dst, send_sem=send_sem.at[i], recv_sem=recv_sem.at[i],
            device_id=device, device_id_type=MESH,
        )

    def load_up(j):
        c = chunk_at(j)
        cols = pl.ds(pl.multiple_of(c * part, part), part)
        return pltpu.make_async_copy(up_in.at[:, cols], up_v.at[c], up_sem.at[j])

    def load_down(j):
        c = chunk_at(j)
        lines = pl.ds(pl.multiple_of(c * part, part), part)
        return pltpu.make_async_copy(down_in.at[lines, :], down_v.at[c], down_sem.at[j])

    small = [
        (mix_in, mix_v.at[group(0)]),
        (gain1_in, gain1_v),
        (gain2_in, gain2_v),
        (grad_in, grad_v),
        (owner_in, owner_v.at[0]),
        (slot_in, slot_v.at[0]),
    ]
    loads = [pltpu.make_async_copy(s, d, load_sem.at[i]) for i, (s, d) in enumerate(small)]
    loads[0].start()
    loads[1].start()
    load_up(0).start()
    load_down(0).start()

    needed = row + col + jnp.minimum(tok, 1)

    @pl.when(needed > 0)
    def _():
        pl.semaphore_wait(barrier, needed)

    @pl.when(tok != 0)
    def _():
        pl.semaphore_signal(ready_sem, inc=1, device_id={"token": 0}, device_id_type=MESH)

    mix_x = remote(0, mix_in, mix_v.at[group(1)], over_x)
    mix_y = remote(1, mix_in, mix_v.at[group(2)], over_y)
    ids = [
        remote(2, owner_in, owner_v.at[1], over_x),
        remote(3, slot_in, slot_v.at[1], over_x),
        remote(4, owner_in, owner_v.at[2], over_y),
        remote(5, slot_in, slot_v.at[2], over_y),
    ]
    @pl.when(col == 1)
    def _():
        pl.semaphore_signal(x_sem, inc=1, device_id=over_x, device_id_type=MESH)
        mix_x.start()

    @pl.when(row == 1)
    def _():
        pl.semaphore_signal(y_sem, inc=1, device_id=over_y, device_id_type=MESH)
        mix_y.start()

    def last_half(k):
        return pl.ds(3 * rows + k * half_r, half_r)

    def norm_group(g):
        normed, _ = normalize(mix_v[group(g), :].astype(f32))
        h_v[group(g), :] = (normed * gain1_v[...]).astype(bf)

    def pick_group(g):
        shape = (hsel_v.shape[0], width)
        line = lax.broadcasted_iota(jnp.int32, shape, 0) + me * shape[0]
        pick = (line == lax.broadcasted_iota(jnp.int32, shape, 1)).astype(bf)
        if g < 3:
            hsel_v[:, group(g)] = contract_cols(pick, h_v[group(g), :]).astype(bf)
        else:
            for k in range(2):
                hlast_v[k] = contract_cols(pick, h_v[last_half(k), :]).astype(bf)

    def activate(g, c):
        pres = [
            contract_flat(h_v[group(g), :], up_v[c, :, s : s + SUB]) for s in range(0, part, SUB)
        ]
        total = None
        for i, pre in enumerate(pres):
            cols = slice(i * SUB, (i + 1) * SUB)
            value, slope = gelu_parts(pre)
            act = value.astype(bf)
            act_v[group(g), cols] = act
            slope_v[c, group(g), cols] = slope.astype(bf)
            if g == 0:
                more = contract_flat(act, down_v[c, cols, :])
                total = more if total is None else total + more
        return total

    loads[0].wait()
    loads[1].wait()
    norm_group(0)
    acc_v[...] = h_v[group(0), :].astype(f32)

    @pl.when(col == 0)
    def _():
        pl.semaphore_wait(x_sem, 1)
        mix_x.start()

    @pl.when(row == 0)
    def _():
        pl.semaphore_wait(y_sem, 1)
        mix_y.start()

    for copy in ids:
        copy.start()

    for j in range(chunks):
        load_up(j).wait()
        load_down(j).wait()
        if j + 1 < chunks:
            load_up(j + 1).start()
            load_down(j + 1).start()
        else:
            for load in loads[2:]:
                load.start()
        acc_v[...] += activate(0, chunk_at(j))

    for load in loads[2:]:
        load.wait()
    normed, inv = normalize(acc_v[...])
    wide = norm_back(grad_v[...].astype(f32) * gain2_v[...], normed, inv)
    wide_v[...] = wide
    mid_v[group(0), :] = wide.astype(bf)
    mid_x = remote(6, mid_v.at[group(0)], mid_v.at[group(1)], over_x)
    mid_y = remote(7, mid_v.at[group(0)], mid_v.at[group(2)], over_y)
    mid_x.start()
    mid_y.start()

    @pl.when(tok == 0)
    def _():
        pl.semaphore_wait(ready_sem, n_tok - 1)
        for k in range(1, n_tok):
            pl.semaphore_signal(go_sem, inc=1, device_id={"token": k}, device_id_type=MESH)

    def slope_lines(lines, c):
        grad_act = contract_cols(mid_v[lines, :], down_v[c])
        grad_pre = (grad_act * slope_v[c, lines, :].astype(f32)).astype(bf)
        slope_v[c, lines, :] = grad_pre
        return grad_pre

    def slope_group(g, c):
        return slope_lines(group(g), c)

    acc_v[...] = wide_v[...]

    @pl.loop(0, chunks, unroll=UNROLL)
    def _(c):
        acc_v[...] += contract_cols(slope_group(0, c), up_v[c])

    normed, inv = normalize(mix_v[group(0), :].astype(f32))
    grad_sum = norm_back(acc_v[...] * gain1_v[...], normed, inv)
    sum_v[...] = grad_sum.T.astype(bf)

    @pl.when(tok != 0)
    def _():
        pl.semaphore_wait(go_sem, 1)

    own_piece = pl.ds(pl.multiple_of(tok * piece, piece), piece)
    swaps = []
    for k in range(1, n_tok):
        peer = lax.rem(tok + k, n_tok)
        there = pl.ds(pl.multiple_of(peer * piece, piece), piece)
        swaps.append(
            pltpu.make_async_remote_copy(
                src_ref=sum_v.at[there], dst_ref=swap_v.at[own_piece],
                send_sem=swap_send.at[k - 1], recv_sem=swap_recv.at[k - 1],
                device_id={"token": peer}, device_id_type=MESH,
            )
        )
        swaps[-1].start()
    swap_v[own_piece, :] = sum_v[own_piece, :]

    first, second = pl.ds(0, half_r), pl.ds(half_r, half_r)

    def block(ref, g, part_of):
        return ref.at[pl.ds(g * rows + part_of * half_r, half_r)]

    mix_x.wait_recv()
    mix_dx = remote(8, block(mix_v, 1, 0), block(mix_v, 3, 0), over_y)
    mix_dx.start()
    mix_y.wait_recv()
    mix_dy = remote(9, block(mix_v, 2, 1), block(mix_v, 3, 1), over_x)
    mix_dy.start()

    def others(g):
        norm_group(g)
        pick_group(g)

        @pl.loop(0, chunks, unroll=UNROLL)
        def _(j):
            activate(g, chunk_at(j))

    pick_group(0)
    others(1)
    others(2)

    def piece_of(g, k):
        return mid_v.at[pl.ds(g * rows + k * (half_r // 2), half_r // 2)]

    mid_x.wait_recv()
    mid_y.wait_recv()
    mid_d = [
        remote(12, piece_of(1, 0), piece_of(3, 0), over_y),
        remote(13, piece_of(2, 1), piece_of(3, 1), over_x),
        remote(16, piece_of(1, 2), piece_of(3, 2), over_y),
        remote(17, piece_of(2, 3), piece_of(3, 3), over_x),
    ]
    mid_d[0].start()
    mid_d[1].start()

    pair = pl.ds(0, 2 * rows)

    @pl.loop(0, chunks, unroll=UNROLL)
    def _(c):
        slope_group(1, c)
        gup_v[c] = contract_flat(hsel_v[:, pair], slope_v[c, pair, :])

    for copy in swaps:
        copy.wait_recv()
    embed_v[...] = (sum_v[...].astype(f32) + swap_v[...].astype(f32)).astype(bf)
    low, high = pl.ds(0, half_w), pl.ds(half_w, half_w)
    far_x = remote(10, embed_v.at[low], far_v.at[0], over_x)
    far_y = remote(11, embed_v.at[high], far_v.at[1], over_y)
    far_x.start()
    far_y.start()
    mid_d[2].start()
    mid_d[3].start()

    gdown_v[...] = contract_rows(act_v[pair, :], mid_v[pair, :])

    @pl.loop(0, chunks, unroll=UNROLL)
    def _(c):
        grad_pre = slope_group(2, c)
        gup_v[c] += contract_flat(hsel_v[:, group(2)], grad_pre)

    gdown_v[...] += contract_rows(act_v[group(2), :], mid_v[group(2), :])

    mix_dx.wait_recv()
    mix_dy.wait_recv()
    others(3)

    def last_group(k):
        lines = last_half(k)

        @pl.loop(0, chunks, unroll=UNROLL)
        def _(c):
            gup_v[c] += contract_flat(hlast_v[k], slope_lines(lines, c))

        gdown_v[...] += contract_rows(act_v[lines, :], mid_v[lines, :])

    mid_d[0].wait_recv()
    mid_d[1].wait_recv()
    last_group(0)

    for copy in ids:
        copy.wait_recv()
    far_x.wait_recv()
    far_y.wait_recv()

    def hot(k, owner):
        target = owner_v[k] * hot_rows + slot_v[k]
        line = lax.broadcasted_iota(jnp.int32, (hot_rows, rows), 0) + owner * hot_rows
        return (line == target).astype(bf)

    def merge(owner, k, cols):
        kept = contract_cols(hot(0, owner), embed_v[cols, :])
        return kept + contract_cols(hot(k, owner), far_v[k - 1])

    part_v[0] = merge(over_y["dp"], 1, low).astype(bf)
    part_v[1] = merge(over_x["dp"], 2, high).astype(bf)
    back_y = remote(14, part_v.at[0], back_v.at[0], over_y)
    back_x = remote(15, part_v.at[1], back_v.at[1], over_x)
    back_y.start()
    back_x.start()
    mine_v[:, :half_w] = merge(me, 1, low)
    mine_v[:, half_w:] = merge(me, 2, high)

    mid_d[2].wait_recv()
    mid_d[3].wait_recv()
    last_group(1)

    back_y.wait_recv()
    back_x.wait_recv()
    mine_v[:, :half_w] += back_v[0].astype(f32)
    mine_v[:, half_w:] += back_v[1].astype(f32)

    for copy in [mix_x, mix_y] + ids + [mid_x, mid_y, mix_dx, mix_dy] + swaps:
        copy.wait_send()
    for copy in [far_x, far_y, back_x, back_y] + mid_d:
        copy.wait_send()


def store_kernel(up_ref, down_ref, rows_ref, up_out, down_out, rows_out, sems):
    chunks, _, part = up_ref.shape
    copies = [
        pltpu.make_async_copy(up_ref.at[c], up_out.at[:, pl.ds(c * part, part)], sems.at[c])
        for c in range(chunks)
    ]
    quarter = part // chunks
    for c in range(chunks):
        lines = pl.ds(c * quarter, quarter)
        copies.append(
            pltpu.make_async_copy(down_ref.at[lines], down_out.at[lines], sems.at[chunks + c])
        )
    copies.append(pltpu.make_async_copy(rows_ref, rows_out, sems.at[2 * chunks]))
    for copy in copies:
        copy.start()
    for copy in copies:
        copy.wait()


def small_group(mix_input, out_grad, w_up, w_down, gain_first, gain_second, owner_dev, slot_row):
    rows = mix_input.shape[0]
    width = mix_input.shape[2]
    hidden = w_up.shape[2]
    groups = lax.axis_size("dp")
    n_tok = lax.axis_size("token")
    part = hidden // groups
    own = width // groups
    half = width // 2
    bf, f32, i32 = jnp.bfloat16, jnp.float32, jnp.int32
    vm, dma = pltpu.VMEM, pltpu.SemaphoreType.DMA
    main = pl.BlockSpec(memory_space=pltpu.HBM)
    inside = pl.BlockSpec(memory_space=pltpu.VMEM)
    unit = 2 * rows * width * hidden
    held = pl.pallas_call(
        functools.partial(fused_kernel, n_tok),
        in_specs=[main] * 8,
        out_specs=[inside] * 3,
        out_shape=[vm((groups, own, part), f32), vm((part, width), f32), vm((HOT, width), f32)],
        scratch_shapes=[
            vm((groups * rows, width), bf),
            vm((groups * rows, width), bf),
            vm((groups * rows, width), bf),
            vm((groups, width, part), bf),
            vm((groups, part, width), bf),
            vm((groups, groups * rows, part), bf),
            vm((groups * rows, part), bf),
            vm((own, (groups - 1) * rows), bf),
            vm((2, own, rows // 2), bf),
            vm((rows, width), f32),
            vm((rows, width), f32),
            vm((rows, width), bf),
            vm((width, rows), bf),
            vm((width, rows), bf),
            vm((width, rows), bf),
            vm((2, half, rows), bf),
            vm((2, HOT, half), bf),
            vm((2, HOT, half), bf),
            vm((1, width), f32),
            vm((1, width), f32),
            vm((3, 1, rows), i32),
            vm((3, 1, rows), i32),
            dma((groups,)),
            dma((groups,)),
            dma((6,)),
            dma((18,)),
            dma((18,)),
            dma((n_tok - 1,)),
            dma((n_tok - 1,)),
            pltpu.SemaphoreType.REGULAR,
            pltpu.SemaphoreType.REGULAR,
            pltpu.SemaphoreType.REGULAR,
            pltpu.SemaphoreType.REGULAR,
        ],
        compiler_params=pltpu.CompilerParams(
            vmem_limit_bytes=VMEM_BYTES, collective_id=0, has_side_effects=True
        ),
        cost_estimate=pl.CostEstimate(
            flops=12 * unit, bytes_accessed=8 * width * hidden, transcendentals=0
        ),
        name="fused",
    )(
        mix_input[:, 0, :], out_grad[:, 0, :], w_up[0], w_down[0], gain_first, gain_second,
        owner_dev[:, :, 0], slot_row,
    )
    grad_up, grad_down, row_grad = pl.pallas_call(
        store_kernel,
        in_specs=[pl.BlockSpec(memory_space=pl.ANY)] * 3,
        out_specs=[main] * 3,
        out_shape=[
            jax.ShapeDtypeStruct((own, hidden), f32),
            jax.ShapeDtypeStruct((part, width), f32),
            jax.ShapeDtypeStruct((HOT, width), f32),
        ],
        scratch_shapes=[dma((2 * groups + 1,))],
        compiler_params=pltpu.CompilerParams(vmem_limit_bytes=1 << 20),
        name="store",
    )(*held)
    return (grad_up[None], grad_down[None], row_grad[None])


def solution(mesh):
    placed = (
        P("dp", "token", None),
        P("dp", "token", None),
        P("token", None, None),
        P("token", None, None),
        P("token", None),
        P("token", None),
        P("token", "dp", None),
        P("token", "dp"),
    )
    small = mesh.shape["dp"] == 4
    return jax.shard_map(
        small_group if small else per_device,
        mesh=mesh,
        in_specs=placed,
        out_specs=(P("token", "dp", None), P("token", "dp", None), P("token", "dp", None)),
        check_vma=False,
    )
```

```python
import functools

import jax
import jax.numpy as jnp
from jax import lax
from jax.experimental import pallas as pl
from jax.experimental.pallas import tpu as pltpu

from jax.sharding import PartitionSpec as P

HOT = 256


EPS = 1e-05
HALF_ROOT = 0.7071067811865476
INV_ROOT_TAU = 0.3989422804014327


def normalize(values):
    center = values - jnp.mean(values, axis=-1, keepdims=True)
    inv_scale = lax.rsqrt(jnp.mean(center * center, axis=-1, keepdims=True) + EPS)
    return (center * inv_scale, inv_scale)


def norm_back(grad_norm, normed, inv_scale):
    mean_grad = jnp.mean(grad_norm, axis=-1, keepdims=True)
    mean_proj = jnp.mean(grad_norm * normed, axis=-1, keepdims=True)
    return inv_scale * (grad_norm - mean_grad - normed * mean_proj)


def gelu_parts(pre_act):
    cumul = 0.5 * (1.0 + jax.scipy.special.erf(pre_act * HALF_ROOT))
    density = jnp.exp(-0.5 * pre_act * pre_act) * INV_ROOT_TAU
    return (pre_act * cumul, cumul + pre_act * density)


def contract_rows(left, right):
    return lax.dot_general(
        left, right, (((0,), (0,)), ((), ())), preferred_element_type=jnp.float32
    )


def contract_cols(left, right):
    return lax.dot_general(
        left, right, (((1,), (1,)), ((), ())), preferred_element_type=jnp.float32
    )


def per_device(mix_input, out_grad, w_up, w_down, gain_first, gain_second, owner_dev, slot_row):
    batch_rows = mix_input.shape[0]
    width = mix_input.shape[2]
    owners = lax.axis_size("dp")
    normed, inv_scale = normalize(mix_input[:, 0, :].astype(jnp.float32))
    hidden_in = (normed * gain_first[0]).astype(jnp.bfloat16)
    pre_act = jnp.dot(hidden_in, w_up[0], preferred_element_type=jnp.float32)
    act_value, act_slope = gelu_parts(pre_act)
    active = act_value.astype(jnp.bfloat16)
    outer_sum = jnp.dot(active, w_down[0], preferred_element_type=jnp.float32) + hidden_in.astype(
        jnp.float32
    )
    normed_out, inv_out = normalize(outer_sum)
    grad_wide = norm_back(
        out_grad[:, 0, :].astype(jnp.float32) * gain_second[0], normed_out, inv_out
    )
    grad_mid = grad_wide.astype(jnp.bfloat16)
    grad_act = contract_cols(grad_mid, w_down[0])
    grad_pre = (grad_act * act_slope).astype(jnp.bfloat16)
    up_whole = contract_rows(hidden_in, grad_pre)
    down_whole = contract_rows(active, grad_mid)
    grad_up, grad_down = (
        lax.psum_scatter(
            up_whole.astype(jnp.bfloat16), "dp", scatter_dimension=0, tiled=True
        ).astype(jnp.float32),
        lax.psum_scatter(
            down_whole.astype(jnp.bfloat16), "dp", scatter_dimension=0, tiled=True
        ).astype(jnp.float32),
    )
    grad_hidden = contract_cols(grad_pre, w_up[0]) + grad_wide
    grad_sum = norm_back(grad_hidden * gain_first[0], normed, inv_scale).astype(jnp.bfloat16)
    pieces = lax.axis_size("token")
    swapped = lax.all_to_all(
        grad_sum.reshape(batch_rows, pieces, width // pieces),
        "token",
        split_axis=1,
        concat_axis=1,
        tiled=True,
    )
    embed_grad = (
        grad_sum.astype(jnp.float32) + swapped.reshape(batch_rows, width).astype(jnp.float32)
    ).astype(jnp.bfloat16)
    owner_ids = owner_dev[0, :, 0]
    slot_ids = slot_row[0]
    capacity = max(2, 8 * (5 * batch_rows // (16 * owners)))
    owner_hot = (
        owner_ids[:, None] == lax.broadcasted_iota(jnp.int32, (batch_rows, owners), 1)
    ).astype(jnp.int32)
    rank_within = jnp.sum((jnp.cumsum(owner_hot, axis=0) - 1) * owner_hot, axis=1)
    place = owner_ids * capacity + rank_within
    dispatch_mask = (
        lax.broadcasted_iota(jnp.int32, (owners * capacity, batch_rows), 0) == place[None, :]
    )
    send_grad = jnp.dot(
        dispatch_mask.astype(jnp.bfloat16), embed_grad, preferred_element_type=jnp.float32
    )
    send_grad = send_grad.astype(jnp.bfloat16).reshape(owners, capacity, width)
    send_slot = jnp.sum(dispatch_mask.astype(jnp.int32) * (slot_ids + 1)[None, :], axis=1) - 1
    send_slot = send_slot.astype(jnp.float32).astype(jnp.bfloat16).reshape(owners, capacity)
    recv_grad, recv_slot = (
        lax.all_to_all(send_grad, "dp", split_axis=0, concat_axis=0, tiled=True),
        lax.all_to_all(send_slot, "dp", split_axis=0, concat_axis=0, tiled=True),
    )
    slot_values = recv_slot.reshape(1, owners * capacity).astype(jnp.float32)
    gather_hot = (
        lax.broadcasted_iota(jnp.int32, (HOT, owners * capacity), 0).astype(jnp.float32)
        == slot_values
    ).astype(jnp.bfloat16)
    row_grad = jnp.dot(
        gather_hot, recv_grad.reshape(owners * capacity, width), preferred_element_type=jnp.float32
    )
    return (grad_up[None], grad_down[None], row_grad[None])


SUB = 256
UNROLL = 4
VMEM_BYTES = 56 * 1024 * 1024
MESH = pl.DeviceIdType.MESH


def contract_flat(left, right):
    return jnp.dot(left, right, preferred_element_type=jnp.float32)


def fused_kernel(
    n_tok,
    mix_in, grad_in, up_in, down_in, gain1_in, gain2_in, owner_in, slot_in,
    gup_v, gdown_v, mine_v,
    mix_v, mid_v, h_v, up_v, down_v, slope_v, act_v, hsel_v, hlast_v, wide_v, acc_v, grad_v,
    sum_v, swap_v, embed_v, far_v, part_v, back_v, gain1_v, gain2_v, owner_v, slot_v,
    up_sem, down_sem, load_sem, send_sem, recv_sem, swap_send, swap_recv, ready_sem, go_sem, x_sem, y_sem,
):
    rows, width = grad_v.shape
    chunks, _, part = up_v.shape
    piece = width // n_tok
    half_w = width // 2
    half_r = rows // 2
    hot_rows = mine_v.shape[0]
    bf, f32 = jnp.bfloat16, jnp.float32
    me = lax.axis_index("dp")
    tok = lax.axis_index("token")
    col = lax.rem(me, 2)
    over_x = {"dp": me + 1 - 2 * col}
    row = me // 2
    over_y = {"dp": lax.rem(me + 2, 4)}

    barrier = pltpu.get_barrier_semaphore()

    @pl.when(col == 0)
    def _():
        pl.semaphore_signal(barrier, inc=1, device_id=over_x, device_id_type=MESH)

    @pl.when(row == 0)
    def _():
        pl.semaphore_signal(barrier, inc=1, device_id=over_y, device_id_type=MESH)

    @pl.when(tok == 0)
    def _():
        for k in range(1, n_tok):
            pl.semaphore_signal(barrier, inc=1, device_id={"token": k}, device_id_type=MESH)

    def group(g):
        return pl.ds(g * rows, rows)

    def chunk_at(j):
        return lax.rem(j + me + 1, chunks)

    def remote(i, src, dst, device):
        return pltpu.make_async_remote_copy(
            src_ref=src, dst_ref=dst, send_sem=send_sem.at[i], recv_sem=recv_sem.at[i],
            device_id=device, device_id_type=MESH,
        )

    def load_up(j):
        c = chunk_at(j)
        cols = pl.ds(pl.multiple_of(c * part, part), part)
        return pltpu.make_async_copy(up_in.at[:, cols], up_v.at[c], up_sem.at[j])

    def load_down(j):
        c = chunk_at(j)
        lines = pl.ds(pl.multiple_of(c * part, part), part)
        return pltpu.make_async_copy(down_in.at[lines, :], down_v.at[c], down_sem.at[j])

    small = [
        (mix_in, mix_v.at[group(0)]),
        (gain1_in, gain1_v),
        (gain2_in, gain2_v),
        (grad_in, grad_v),
        (owner_in, owner_v.at[0]),
        (slot_in, slot_v.at[0]),
    ]
    loads = [pltpu.make_async_copy(s, d, load_sem.at[i]) for i, (s, d) in enumerate(small)]
    loads[0].start()
    loads[1].start()
    load_up(0).start()
    load_down(0).start()

    needed = row + col + jnp.minimum(tok, 1)

    @pl.when(needed > 0)
    def _():
        pl.semaphore_wait(barrier, needed)

    @pl.when(tok != 0)
    def _():
        pl.semaphore_signal(ready_sem, inc=1, device_id={"token": 0}, device_id_type=MESH)

    mix_x = remote(0, mix_in, mix_v.at[group(1)], over_x)
    mix_y = remote(1, mix_in, mix_v.at[group(2)], over_y)
    ids = [
        remote(2, owner_in, owner_v.at[1], over_x),
        remote(3, slot_in, slot_v.at[1], over_x),
        remote(4, owner_in, owner_v.at[2], over_y),
        remote(5, slot_in, slot_v.at[2], over_y),
    ]
    @pl.when(col == 1)
    def _():
        pl.semaphore_signal(x_sem, inc=1, device_id=over_x, device_id_type=MESH)
        mix_x.start()

    @pl.when(row == 1)
    def _():
        pl.semaphore_signal(y_sem, inc=1, device_id=over_y, device_id_type=MESH)
        mix_y.start()

    def last_half(k):
        return pl.ds(3 * rows + k * half_r, half_r)

    def norm_group(g):
        normed, _ = normalize(mix_v[group(g), :].astype(f32))
        h_v[group(g), :] = (normed * gain1_v[...]).astype(bf)

    def pick_group(g):
        shape = (hsel_v.shape[0], width)
        line = lax.broadcasted_iota(jnp.int32, shape, 0) + me * shape[0]
        pick = (line == lax.broadcasted_iota(jnp.int32, shape, 1)).astype(bf)
        if g < 3:
            hsel_v[:, group(g)] = contract_cols(pick, h_v[group(g), :]).astype(bf)
        else:
            for k in range(2):
                hlast_v[k] = contract_cols(pick, h_v[last_half(k), :]).astype(bf)

    def activate(g, c):
        pres = [
            contract_flat(h_v[group(g), :], up_v[c, :, s : s + SUB]) for s in range(0, part, SUB)
        ]
        total = None
        for i, pre in enumerate(pres):
            cols = slice(i * SUB, (i + 1) * SUB)
            value, slope = gelu_parts(pre)
            act = value.astype(bf)
            act_v[group(g), cols] = act
            slope_v[c, group(g), cols] = slope.astype(bf)
            if g == 0:
                more = contract_flat(act, down_v[c, cols, :])
                total = more if total is None else total + more
        return total

    loads[0].wait()
    loads[1].wait()
    norm_group(0)
    acc_v[...] = h_v[group(0), :].astype(f32)

    @pl.when(col == 0)
    def _():
        pl.semaphore_wait(x_sem, 1)
        mix_x.start()

    @pl.when(row == 0)
    def _():
        pl.semaphore_wait(y_sem, 1)
        mix_y.start()

    for copy in ids:
        copy.start()

    for j in range(chunks):
        load_up(j).wait()
        load_down(j).wait()
        if j + 1 < chunks:
            load_up(j + 1).start()
            load_down(j + 1).start()
        else:
            for load in loads[2:]:
                load.start()
        acc_v[...] += activate(0, chunk_at(j))

    for load in loads[2:]:
        load.wait()
    normed, inv = normalize(acc_v[...])
    wide = norm_back(grad_v[...].astype(f32) * gain2_v[...], normed, inv)
    wide_v[...] = wide
    mid_v[group(0), :] = wide.astype(bf)
    mid_x = remote(6, mid_v.at[group(0)], mid_v.at[group(1)], over_x)
    mid_y = remote(7, mid_v.at[group(0)], mid_v.at[group(2)], over_y)
    mid_x.start()
    mid_y.start()

    @pl.when(tok == 0)
    def _():
        pl.semaphore_wait(ready_sem, n_tok - 1)
        for k in range(1, n_tok):
            pl.semaphore_signal(go_sem, inc=1, device_id={"token": k}, device_id_type=MESH)

    def slope_lines(lines, c):
        grad_act = contract_cols(mid_v[lines, :], down_v[c])
        grad_pre = (grad_act * slope_v[c, lines, :].astype(f32)).astype(bf)
        slope_v[c, lines, :] = grad_pre
        return grad_pre

    def slope_group(g, c):
        return slope_lines(group(g), c)

    acc_v[...] = wide_v[...]

    @pl.loop(0, chunks, unroll=UNROLL)
    def _(c):
        acc_v[...] += contract_cols(slope_group(0, c), up_v[c])

    normed, inv = normalize(mix_v[group(0), :].astype(f32))
    grad_sum = norm_back(acc_v[...] * gain1_v[...], normed, inv)
    sum_v[...] = grad_sum.T.astype(bf)

    @pl.when(tok != 0)
    def _():
        pl.semaphore_wait(go_sem, 1)

    own_piece = pl.ds(pl.multiple_of(tok * piece, piece), piece)
    swaps = []
    for k in range(1, n_tok):
        peer = lax.rem(tok + k, n_tok)
        there = pl.ds(pl.multiple_of(peer * piece, piece), piece)
        swaps.append(
            pltpu.make_async_remote_copy(
                src_ref=sum_v.at[there], dst_ref=swap_v.at[own_piece],
                send_sem=swap_send.at[k - 1], recv_sem=swap_recv.at[k - 1],
                device_id={"token": peer}, device_id_type=MESH,
            )
        )
        swaps[-1].start()
    swap_v[own_piece, :] = sum_v[own_piece, :]

    first, second = pl.ds(0, half_r), pl.ds(half_r, half_r)

    def block(ref, g, part_of):
        return ref.at[pl.ds(g * rows + part_of * half_r, half_r)]

    mix_x.wait_recv()
    mix_dx = remote(8, block(mix_v, 1, 0), block(mix_v, 3, 0), over_y)
    mix_dx.start()
    mix_y.wait_recv()
    mix_dy = remote(9, block(mix_v, 2, 1), block(mix_v, 3, 1), over_x)
    mix_dy.start()

    def others(g):
        norm_group(g)
        pick_group(g)

        @pl.loop(0, chunks, unroll=UNROLL)
        def _(j):
            activate(g, chunk_at(j))

    pick_group(0)
    others(1)
    others(2)

    def piece_of(g, k):
        return mid_v.at[pl.ds(g * rows + k * (half_r // 2), half_r // 2)]

    mid_x.wait_recv()
    mid_y.wait_recv()
    mid_d = [
        remote(12, piece_of(1, 0), piece_of(3, 0), over_y),
        remote(13, piece_of(2, 1), piece_of(3, 1), over_x),
        remote(16, piece_of(1, 2), piece_of(3, 2), over_y),
        remote(17, piece_of(2, 3), piece_of(3, 3), over_x),
    ]
    mid_d[0].start()
    mid_d[1].start()

    pair = pl.ds(0, 2 * rows)

    @pl.loop(0, chunks, unroll=UNROLL)
    def _(c):
        slope_group(1, c)
        gup_v[c] = contract_flat(hsel_v[:, pair], slope_v[c, pair, :])

    for copy in swaps:
        copy.wait_recv()
    embed_v[...] = (sum_v[...].astype(f32) + swap_v[...].astype(f32)).astype(bf)
    low, high = pl.ds(0, half_w), pl.ds(half_w, half_w)
    far_x = remote(10, embed_v.at[low], far_v.at[0], over_x)
    far_y = remote(11, embed_v.at[high], far_v.at[1], over_y)
    far_x.start()
    far_y.start()

    gdown_v[...] = contract_rows(act_v[pair, :], mid_v[pair, :])

    @pl.loop(0, chunks, unroll=UNROLL)
    def _(c):
        grad_pre = slope_group(2, c)
        gup_v[c] += contract_flat(hsel_v[:, group(2)], grad_pre)

    gdown_v[...] += contract_rows(act_v[group(2), :], mid_v[group(2), :])

    mid_d[2].start()
    mid_d[3].start()
    mix_dx.wait_recv()
    mix_dy.wait_recv()
    others(3)

    def last_group(k):
        lines = last_half(k)

        @pl.loop(0, chunks, unroll=UNROLL)
        def _(c):
            gup_v[c] += contract_flat(hlast_v[k], slope_lines(lines, c))

        gdown_v[...] += contract_rows(act_v[lines, :], mid_v[lines, :])

    mid_d[0].wait_recv()
    mid_d[1].wait_recv()
    last_group(0)

    for copy in ids:
        copy.wait_recv()
    far_x.wait_recv()
    far_y.wait_recv()

    def hot(k, owner):
        target = owner_v[k] * hot_rows + slot_v[k]
        line = lax.broadcasted_iota(jnp.int32, (hot_rows, rows), 0) + owner * hot_rows
        return (line == target).astype(bf)

    def merge(owner, k, cols):
        kept = contract_cols(hot(0, owner), embed_v[cols, :])
        return kept + contract_cols(hot(k, owner), far_v[k - 1])

    part_v[0] = merge(over_y["dp"], 1, low).astype(bf)
    part_v[1] = merge(over_x["dp"], 2, high).astype(bf)
    back_y = remote(14, part_v.at[0], back_v.at[0], over_y)
    back_x = remote(15, part_v.at[1], back_v.at[1], over_x)
    back_y.start()
    back_x.start()
    mine_v[:, :half_w] = merge(me, 1, low)
    mine_v[:, half_w:] = merge(me, 2, high)

    mid_d[2].wait_recv()
    mid_d[3].wait_recv()
    last_group(1)

    for copy in [mix_x, mix_y] + ids + [mid_x, mid_y, mix_dx, mix_dy] + swaps:
        copy.wait_send()
    back_y.wait_recv()
    mine_v[:, :half_w] += back_v[0].astype(f32)
    back_x.wait_recv()
    mine_v[:, half_w:] += back_v[1].astype(f32)

    for copy in [far_x, far_y, back_x, back_y] + mid_d:
        copy.wait_send()


def store_kernel(up_ref, down_ref, rows_ref, up_out, down_out, rows_out, sems):
    chunks, _, part = up_ref.shape
    copies = [
        pltpu.make_async_copy(up_ref.at[c], up_out.at[:, pl.ds(c * part, part)], sems.at[c])
        for c in range(chunks)
    ]
    quarter = part // chunks
    for c in range(chunks):
        lines = pl.ds(c * quarter, quarter)
        copies.append(
            pltpu.make_async_copy(down_ref.at[lines], down_out.at[lines], sems.at[chunks + c])
        )
    copies.append(pltpu.make_async_copy(rows_ref, rows_out, sems.at[2 * chunks]))
    for copy in copies:
        copy.start()
    for copy in copies:
        copy.wait()


def small_group(mix_input, out_grad, w_up, w_down, gain_first, gain_second, owner_dev, slot_row):
    rows = mix_input.shape[0]
    width = mix_input.shape[2]
    hidden = w_up.shape[2]
    groups = lax.axis_size("dp")
    n_tok = lax.axis_size("token")
    part = hidden // groups
    own = width // groups
    half = width // 2
    bf, f32, i32 = jnp.bfloat16, jnp.float32, jnp.int32
    vm, dma = pltpu.VMEM, pltpu.SemaphoreType.DMA
    main = pl.BlockSpec(memory_space=pltpu.HBM)
    inside = pl.BlockSpec(memory_space=pltpu.VMEM)
    unit = 2 * rows * width * hidden
    held = pl.pallas_call(
        functools.partial(fused_kernel, n_tok),
        in_specs=[main] * 8,
        out_specs=[inside] * 3,
        out_shape=[vm((groups, own, part), f32), vm((part, width), f32), vm((HOT, width), f32)],
        scratch_shapes=[
            vm((groups * rows, width), bf),
            vm((groups * rows, width), bf),
            vm((groups * rows, width), bf),
            vm((groups, width, part), bf),
            vm((groups, part, width), bf),
            vm((groups, groups * rows, part), bf),
            vm((groups * rows, part), bf),
            vm((own, (groups - 1) * rows), bf),
            vm((2, own, rows // 2), bf),
            vm((rows, width), f32),
            vm((rows, width), f32),
            vm((rows, width), bf),
            vm((width, rows), bf),
            vm((width, rows), bf),
            vm((width, rows), bf),
            vm((2, half, rows), bf),
            vm((2, HOT, half), bf),
            vm((2, HOT, half), bf),
            vm((1, width), f32),
            vm((1, width), f32),
            vm((3, 1, rows), i32),
            vm((3, 1, rows), i32),
            dma((groups,)),
            dma((groups,)),
            dma((6,)),
            dma((18,)),
            dma((18,)),
            dma((n_tok - 1,)),
            dma((n_tok - 1,)),
            pltpu.SemaphoreType.REGULAR,
            pltpu.SemaphoreType.REGULAR,
            pltpu.SemaphoreType.REGULAR,
            pltpu.SemaphoreType.REGULAR,
        ],
        compiler_params=pltpu.CompilerParams(
            vmem_limit_bytes=VMEM_BYTES, collective_id=0, has_side_effects=True
        ),
        cost_estimate=pl.CostEstimate(
            flops=12 * unit, bytes_accessed=8 * width * hidden, transcendentals=0
        ),
        name="fused",
    )(
        mix_input[:, 0, :], out_grad[:, 0, :], w_up[0], w_down[0], gain_first, gain_second,
        owner_dev[:, :, 0], slot_row,
    )
    grad_up, grad_down, row_grad = pl.pallas_call(
        store_kernel,
        in_specs=[pl.BlockSpec(memory_space=pl.ANY)] * 3,
        out_specs=[main] * 3,
        out_shape=[
            jax.ShapeDtypeStruct((own, hidden), f32),
            jax.ShapeDtypeStruct((part, width), f32),
            jax.ShapeDtypeStruct((HOT, width), f32),
        ],
        scratch_shapes=[dma((2 * groups + 1,))],
        compiler_params=pltpu.CompilerParams(vmem_limit_bytes=1 << 20),
        name="store",
    )(*held)
    return (grad_up[None], grad_down[None], row_grad[None])


def solution(mesh):
    placed = (
        P("dp", "token", None),
        P("dp", "token", None),
        P("token", None, None),
        P("token", None, None),
        P("token", None),
        P("token", None),
        P("token", "dp", None),
        P("token", "dp"),
    )
    small = mesh.shape["dp"] == 4
    return jax.shard_map(
        small_group if small else per_device,
        mesh=mesh,
        in_specs=placed,
        out_specs=(P("token", "dp", None), P("token", "dp", None), P("token", "dp", None)),
        check_vma=False,
    )
```
